256 devices in a mesh: lat: 8 (over y, z_hi), lon: 32 (over x, z_lo, core).
Axes of the slice: x: 4, y: 4, z: 8 (z_hi: 2, z_lo: 4; z = z_hi * 4 + z_lo), core: 2. Of those that a mesh axis runs over, the one named last changes fastest.
Arguments:
- sea_level: float32 [4096, 1024], P('lon', 'lat'), may hold values from -1 to 5
- east_velocity: float32 [4096, 1024], P('lon', 'lat'), may hold values from -6 to 6
- north_velocity: float32 [4096, 1024], P('lon', 'lat'), may hold values from -6 to 6
- depth: float32 [4096, 1024], P('lon', 'lat'), may hold values from 0.25 to 1
- land_mask: int32 [4096, 1024], P('lon', 'lat'), may hold values from 0 to 1, as said below
- wet_counts: int32 [8, 32], replicated, may hold values from 1 to 16384, as said below
- loading_prev: float32 [4096, 1024], P('lon', 'lat'), may hold values from -4 to 4
- tide_amp: float32 [8], replicated, may hold values from 0.3 to 1
- tide_phase: float32 [8], replicated, may hold values from -3.140625 to 3.140625
- legendre: bfloat16 [1024, 1024, 1024], P('lon', None, 'lat'), may hold values from -0.1875 to 0.1875
- love_factor: float32 [1024], replicated, may hold values from 0.05 to 1
Outputs:
- height_new: float32 [4096, 1024], P('lon', 'lat')
- east_new: float32 [4096, 1024], P('lon', 'lat')
- north_new: float32 [4096, 1024], P('lon', 'lat')
- self_attraction: float32 [4096, 1024], P('lon', 'lat')
The draws below stay inside these ranges and needn't reach their ends.
Inputs may be any that keep to these rules, and one draw needn't show every extreme that they name: `land_mask`: every tile of 128 columns by 128 rows holds at least one wet column, and one tile is wholly wet. wet_counts[p, q] is the number of wet columns of land_mask in latitude band p and longitude band q.
All inputs are finite; a program needn't handle non-finite values.
Results may differ from the reference program's by a relative error of at most 0.0038.
Values may be sent and summed in bfloat16 or wider, within the bound.
A program may use at most 64 MiB of HBM per device.

```python
import math
import jax
import jax.numpy as jnp
from jax import lax

LON_DEV = 128
LAT_DEV = 128
NDEG = 1024
SUBSTEPS = 4
CONSTITUENTS = 8
NLON = 4096
NLAT = 1024
M = 1024
BANDS_LON = 32
BANDS_LAT = 8


def draw_sea_level(key, part):
    rows = lax.broadcasted_iota(jnp.int32, (NLON, NLAT), 1).astype(jnp.float32)
    base = 1.0 + 2.0 * rows / NLAT
    noise = jnp.clip(jax.random.normal(key, (NLON, NLAT), jnp.float32), -4.0, 4.0)
    return base + 0.5 * noise


def wet_table(key):
    values = jax.random.randint(jax.random.fold_in(key, 7), (NLON, NLAT), 0, 5)
    full_lon = jax.random.randint(jax.random.fold_in(key, 11), (), 0, BANDS_LON)
    full_lat = jax.random.randint(jax.random.fold_in(key, 13), (), 0, BANDS_LAT)
    columns = lax.broadcasted_iota(jnp.int32, (NLON, NLAT), 0)
    rows = lax.broadcasted_iota(jnp.int32, (NLON, NLAT), 1)
    anchor = (columns % LON_DEV == 0) & (rows % LAT_DEV == 0)
    full = (columns // LON_DEV == full_lon) & (rows // LAT_DEV == full_lat)
    return jnp.where((values > 0) | anchor | full, 1, 0).astype(jnp.int32)


def draw_land_mask(key, part):
    return wet_table(key)


def draw_wet_counts(key, part):
    table = wet_table(key)
    tiles = jnp.sum(table.reshape(BANDS_LON, LON_DEV, BANDS_LAT, LAT_DEV), axis=(1, 3))
    return tiles.T.astype(jnp.int32)


def block_levels(own_key, extent, shards, least, top_value):
    def one(dim, parts):
        heights = jax.random.uniform(jax.random.fold_in(jax.random.fold_in(own_key, 6), dim), (parts,), jnp.float32, least / len(shards), top_value / len(shards))
        return jnp.repeat(jnp.exp(heights), extent[dim] // parts).reshape((-1,) + (1,) * (len(extent) - dim - 1))

    gain = one(*shards[0])
    for cut in shards[1:]:
        gain = gain * one(*cut)
    return gain


def gaussian(rng, dims, width, reach, cuts=(), kind=jnp.bfloat16):
    array = jax.random.normal(rng, dims, jnp.float32) * width
    if len(cuts) > 0:
        array = block_levels(rng, dims, cuts, -0.22, 0.18) * array
    return jnp.clip(array, min=-reach, max=reach).astype(kind)


def setup_inputs(seed: int = 0) -> dict:
    splits = jax.random.split(jax.random.key(seed), 12)
    sea_level = draw_sea_level(jax.random.fold_in(splits[11], 71), 0)
    east_velocity = gaussian(splits[1], (NLON, NLAT), 1.0, 6.0, ((0, 32), (1, 8)), jnp.float32)
    north_velocity = gaussian(splits[2], (NLON, NLAT), 1.0, 6.0, ((0, 32), (1, 8)), jnp.float32)
    depth = jnp.clip(jnp.exp(math.log(1.0) - 1.3862944 * jax.random.uniform(splits[3], (NLON, NLAT), jnp.float32) ** block_levels(splits[3], (NLON, NLAT), ((0, 32), (1, 8)), -0.2, 0.2)), 0.25, 1.0)
    land_mask = draw_land_mask(jax.random.fold_in(splits[11], 71), 0)
    wet_counts = draw_wet_counts(jax.random.fold_in(splits[11], 71), 0)
    loading_prev = gaussian(splits[6], (NLON, NLAT), 0.5, 4.0, ((0, 32), (1, 8)), jnp.float32)
    tide_amp = jnp.clip(jnp.exp(jax.random.uniform(splits[7], (CONSTITUENTS,), jnp.float32, math.log(0.3), math.log(1.0))), 0.3, 1.0)
    tide_phase = jnp.clip(jax.random.uniform(splits[8], (CONSTITUENTS,), jnp.float32, -3.140625, 3.140625), -3.140625, 3.140625)
    legendre = gaussian(splits[9], (M, NDEG, NLAT), NLAT ** -0.5, 0.1875, ((0, 32), (2, 8)))
    love_factor = jnp.clip(jnp.exp(jax.random.uniform(splits[10], (NDEG,), jnp.float32, math.log(0.05), math.log(1.0))), 0.05, 1.0)
    return dict(sea_level=sea_level, east_velocity=east_velocity, north_velocity=north_velocity, depth=depth, land_mask=land_mask, wet_counts=wet_counts, loading_prev=loading_prev, tide_amp=tide_amp, tide_phase=tide_phase, legendre=legendre, love_factor=love_factor)


lat_edge = 1.3089969
courant = 0.4
friction = 0.02
rotation = 0.2
frequencies = (0.1405, 0.1454, 0.1379, 0.1458, 0.0729, 0.0676, 0.0725, 0.0649)
orders = (2, 2, 2, 2, 1, 1, 1, 1)

def latitude_of(rows, total_rows):
    return -lat_edge + 2.0 * lat_edge * (rows.astype(jnp.float32) + 0.5) / total_rows

def potential(columns, rows, moment, total_cols, total_rows, tide_amp, tide_phase):
    longitude = (2.0 * math.pi * (columns % total_cols).astype(jnp.float32) / total_cols)[:, None]
    latitude = latitude_of(rows, total_rows)[None, :]
    semi = jnp.cos(latitude) ** 2
    diurnal = jnp.sin(2.0 * latitude)
    field = jnp.zeros((columns.shape[0], rows.shape[0]), jnp.float32)
    for index in range(len(frequencies)):
        shape_term = semi if orders[index] == 2 else diurnal
        field = field + tide_amp[index] * shape_term * jnp.cos(frequencies[index] * moment + orders[index] * longitude + tide_phase[index])
    return field * (total_cols / 64.0)

def advance(state_x, static_x, forcing, latitude_x):
    height_x, east_x, north_x = (state_x[0], state_x[1], state_x[2])
    depth_x, wet_x, loading_x = (static_x[0], static_x[1], static_x[2])
    cosine = jnp.cos(latitude_x)[None, :]
    secant_cycle = (1.0 / jnp.cos(latitude_x[1:-1]))[None, :]
    secant_core = (1.0 / jnp.cos(latitude_x[2:-2]))[None, :]
    coriolis = (rotation * jnp.sin(latitude_x[2:-2]))[None, :]
    flux_east = depth_x * east_x
    flux_north = depth_x * north_x * cosine
    divergence = (flux_east[2:, 1:-1] - flux_east[:-2, 1:-1] + (flux_north[1:-1, 2:] - flux_north[1:-1, :-2])) * 0.5 * secant_cycle
    height_cycle = height_x[1:-1, 1:-1] - courant * divergence * wet_x[1:-1, 1:-1]
    pressure = height_cycle - forcing - loading_x[1:-1, 1:-1]
    slope_east = (pressure[2:, 1:-1] - pressure[:-2, 1:-1]) * 0.5 * secant_core
    slope_north = (pressure[1:-1, 2:] - pressure[1:-1, :-2]) * 0.5
    east = east_x[2:-2, 2:-2]
    north = north_x[2:-2, 2:-2]
    wet = wet_x[2:-2, 2:-2]
    east_next = wet * ((1.0 - friction) * east + courant * (coriolis * north - slope_east))
    north_next = wet * ((1.0 - friction) * north - courant * (coriolis * east + slope_north))
    return jnp.stack([height_cycle[1:-1, 1:-1], east_next, north_next])

def extend_grid(fields):
    wide = jnp.pad(fields, ((0, 0), (2, 2), (0, 0)), mode='wrap')
    return jnp.pad(wide, ((0, 0), (0, 0), (2, 2)))

def reference(sea_level, east_velocity, north_velocity, depth, land_mask, wet_counts, loading_prev, tide_amp, tide_phase, legendre, love_factor):
    wet = land_mask.astype(jnp.float32)
    static_x = extend_grid(jnp.stack([depth, wet, loading_prev]))
    state = jnp.stack([sea_level, east_velocity, north_velocity])
    latitude_x = latitude_of(jnp.arange(-2, NLAT + 2, dtype=jnp.int32), NLAT)
    columns = jnp.arange(-1, NLON + 1, dtype=jnp.int32)
    rows = jnp.arange(-1, NLAT + 1, dtype=jnp.int32)
    for moment in range(SUBSTEPS):
        forcing = potential(columns, rows, float(moment), NLON, NLAT, tide_amp, tide_phase)
        state = advance(extend_grid(state), static_x, forcing, latitude_x)
    height = state[0]
    mean_level = jnp.sum(wet * height) / jnp.sum(wet_counts.astype(jnp.float32))
    anomaly = wet * (height - mean_level)
    spectrum = jnp.fft.rfft(anomaly, axis=0)[:M] / math.sqrt(NLON)
    fourier = jnp.stack([jnp.real(spectrum), jnp.imag(spectrum)], axis=1).astype(jnp.bfloat16)

    def one_wave(pair):
        table, wave = pair
        coefficients = jnp.dot(wave, table.T, preferred_element_type=jnp.float32)
        scaled = (coefficients * love_factor[None, :]).astype(jnp.bfloat16)
        return jnp.dot(scaled, table, preferred_element_type=jnp.float32)
    synthesis = lax.map(one_wave, (legendre, fourier))
    padded = jnp.pad(synthesis, ((0, NLON // 2 + 1 - M), (0, 0), (0, 0)))
    spectral = lax.complex(padded[:, 0], padded[:, 1])
    self_attraction = (jnp.fft.irfft(spectral, n=NLON, axis=0) * math.sqrt(NLON)).astype(jnp.float32)
    return (state[0], state[1], state[2], self_attraction)
```

```python
import functools
import math

import jax
import jax.numpy as jnp
import ml_dtypes
import numpy as np
from jax import lax
from jax.experimental import pallas as pl
from jax.experimental.pallas import tpu as pltpu
from jax.sharding import PartitionSpec as P

SUBSTEPS = 4
NLON = 4096
NLAT = 1024
NDEG = 1024
LONS = 32
LATS = 8
TILE = 128
WAVES = 32
ROWS = TILE // LONS
MARGIN = 8
WIDE = TILE + 2 * MARGIN
FIELDS = 6

lat_edge = 1.3089969
courant = 0.4
friction = 0.02
rotation = 0.2
frequencies = (0.1405, 0.1454, 0.1379, 0.1458, 0.0729, 0.0676, 0.0725, 0.0649)
orders = (2, 2, 2, 2, 1, 1, 1, 1)
highest = lax.Precision.HIGHEST
MESH = pl.DeviceIdType.MESH
f32 = jnp.float32
bf16 = jnp.bfloat16


def turn(product, period):
    angle = 2.0 * np.pi * (product % period) / period
    return np.cos(angle), np.sin(angle)


def make_tables():
    band = np.arange(32)
    cell = np.arange(128)
    cos, sin = turn(np.outer(band, band), 32)
    first = np.zeros((8, 2, 32, 32, 8))
    for row in range(8):
        first[row, 0, :, :, row] = cos
        first[row, 1, :, :, row] = -sin
    first = first.reshape(512, 256)
    cos, sin = turn(np.outer(band, cell), 4096)
    twist = np.stack([cos, sin])
    cos, sin = turn(np.outer(band, cell), 128)
    second = np.zeros((32, 8, 2, 2, 128))
    for kind in range(2):
        second[:, 2 * kind, kind, 0] = cos / 64.0
        second[:, 2 * kind, kind, 1] = sin / 64.0
        second[:, 2 * kind + 1, kind, 0] = -sin / 64.0
        second[:, 2 * kind + 1, kind, 1] = cos / 64.0
    second = second.reshape(256, 512)
    place = np.zeros((32, 8, 4, 2, 128))
    spread = np.zeros((32, 2, 4, 2, 128))
    for s in range(32):
        for row in range(4):
            for r in range(2):
                place[s, r, row, r, 4 * s + row] = 1.0
                spread[s, r, row, r, 4 * s + row] = 1.0
    place = place.reshape(256, 1024)
    spread = spread.reshape(64, 1024)
    cos, sin = turn(np.outer(cell, band), 128)
    back = np.zeros((2, 128, 32, 2))
    back[0, :, :, 0] = cos
    back[0, :, :, 1] = -sin
    back[1, :, :, 0] = sin
    back[1, :, :, 1] = cos
    back = back.reshape(256, 64)
    cos, sin = turn(np.outer(cell, band), 4096)
    untwist = np.stack([np.tile(cos, (1, 4)), np.tile(sin, (1, 4))])
    cos, sin = turn(np.outer(band, band), 32)
    last = np.zeros((32, 4, 2, 4, 32))
    for row in range(4):
        last[:, row, 0, row, :] = cos
        last[:, row, 1, row, :] = -sin
    last = last.reshape(128, 256)
    wide = [first, twist, second, back, untwist, last]
    return [x.astype(np.float32) for x in wide] + [
        x.astype(ml_dtypes.bfloat16) for x in (place, spread)
    ]


def stencil(fields, la, north_table, tide):
    h, u, v, depth, wet, loading = fields
    cos, sec, coriolis, semi, diurnal = north_table

    def up(x, axis):
        return pltpu.roll(x, x.shape[axis] - 1, axis)

    def down(x, axis):
        return pltpu.roll(x, 1, axis)

    for moment in range(SUBSTEPS):
        forcing = semi * tide[moment][0] + diurnal * tide[moment][1]
        flux_east = depth * u
        flux_north = depth * v * cos
        divergence = (
            (up(flux_east, 0) - down(flux_east, 0) + (up(flux_north, 1) - down(flux_north, 1)))
            * 0.5
            * sec
        )
        h = h - courant * divergence * wet
        pressure = h - forcing - loading
        slope_east = (up(pressure, 0) - down(pressure, 0)) * 0.5 * sec
        slope_north = (up(pressure, 1) - down(pressure, 1)) * 0.5
        u, v = (
            wet * ((1.0 - friction) * u + courant * (coriolis * v - slope_east)),
            wet * ((1.0 - friction) * v - courant * (coriolis * u + slope_north)),
        )
    return h, u, v


def kernel(
    sea_ref, east_ref, north_ref, depth_ref, mask_ref, load_ref, tide_ref, counts_ref, love_ref,
    leg_hbm, first_hbm, twist_hbm, second_hbm, back_hbm, untwist_hbm, last_hbm, place_hbm, spread_hbm,
    h_out, u_out, v_out, s_out,
    leg, first, twist, second, back, untwist, last, place, spread,
    up_send, dn_send, lo_recv, hi_recv, lf_send, rt_send, lf_recv, rt_recv, dg_send, dg_recv, turned,
    sum_send, sum_recv, a1s, a1r, a2s, a2r, cs, cr, sg, a3s, a3r, a4s, a4r,
    local_sem, halo_send, halo_recv, many_send, many_recv,
):
    la = lax.axis_index("lat")
    lo = lax.axis_index("lon")

    def at(lat, lon):
        return {"lat": lat % LATS, "lon": lon % LONS}

    pairs = (
        (leg_hbm, leg), (first_hbm, first), (twist_hbm, twist), (second_hbm, second), (back_hbm, back),
        (untwist_hbm, untwist), (last_hbm, last), (place_hbm, place), (spread_hbm, spread),
    )
    loads = [
        pltpu.make_async_copy(src, dst, local_sem.at[i]) for i, (src, dst) in enumerate(pairs)
    ]

    barrier = pltpu.get_barrier_semaphore()

    def greet_lon(j, carry):
        pl.semaphore_signal(barrier, inc=1, device_id=at(la, lo + j), device_id_type=MESH)
        return carry

    def greet_lat(j, carry):
        pl.semaphore_signal(barrier, inc=1, device_id=at(la + j, lo), device_id_type=MESH)
        return carry

    lax.fori_loop(1, LATS, greet_lat, 0)
    for dl in (1, LATS - 1):
        for dn in (1, LONS - 1):
            pl.semaphore_signal(barrier, inc=1, device_id=at(la + dl, lo + dn), device_id_type=MESH)
    lax.fori_loop(1, LONS, greet_lon, 0)
    for load in loads:
        load.start()

    wet_core = mask_ref[...].astype(f32)
    cores = [sea_ref[...], east_ref[...], north_ref[...], depth_ref[...], wet_core, load_ref[...]]
    lane = lax.broadcasted_iota(jnp.int32, (TILE, TILE), 1)
    packed = jnp.zeros((TILE, TILE), f32)
    for f in range(FIELDS):
        moved = pltpu.roll(cores[f], 16 * f + 8, 1)
        packed = jnp.where((lane >= 16 * f) & (lane < 16 * f + 16), moved, packed)
        lf_send[f] = cores[f][0:8]
        rt_send[f] = cores[f][TILE - 8 : TILE]
    dg_send[0] = packed[0:8]
    dg_send[1] = packed[TILE - 8 : TILE]
    packed_t = packed.T
    for f in range(FIELDS):
        up_send[8 * f : 8 * f + 8] = packed_t[16 * f : 16 * f + 8]
        dn_send[8 * f : 8 * f + 8] = packed_t[16 * f + 8 : 16 * f + 16]

    pl.semaphore_wait(barrier, LONS - 1 + LATS - 1 + 4)

    moves = (
        (up_send, lo_recv, at(la + 1, lo)),
        (dn_send, hi_recv, at(la + LATS - 1, lo)),
        (lf_send, rt_recv, at(la, lo + LONS - 1)),
        (rt_send, lf_recv, at(la, lo + 1)),
        (dg_send.at[0], dg_recv.at[1, 0], at(la + 1, lo + LONS - 1)),
        (dg_send.at[0], dg_recv.at[1, 1], at(la + LATS - 1, lo + LONS - 1)),
        (dg_send.at[1], dg_recv.at[0, 0], at(la + 1, lo + 1)),
        (dg_send.at[1], dg_recv.at[0, 1], at(la + LATS - 1, lo + 1)),
    )
    halo = [
        pltpu.make_async_remote_copy(
            src_ref=src, dst_ref=dst, send_sem=halo_send.at[i], recv_sem=halo_recv.at[i],
            device_id=dev, device_id_type=MESH,
        )
        for i, (src, dst, dev) in enumerate(moves)
    ]
    for move in halo:
        move.start()

    slot = lax.broadcasted_iota(jnp.int32, (1, 2 * TILE), 1)
    row = la * TILE + jnp.where(slot < 192, slot, slot - 256)
    phi = -lat_edge + 2.0 * lat_edge * (row.astype(f32) + 0.5) / NLAT
    phi = jnp.clip(phi, -1.5, 1.5)
    cos = jnp.cos(phi)
    sec = 1.0 / cos
    coriolis = rotation * jnp.sin(phi)
    semi = cos * cos * (NLON / 64.0)
    diurnal = jnp.sin(2.0 * phi) * (NLON / 64.0)
    column = lo * TILE + lax.broadcasted_iota(jnp.int32, (WIDE, TILE), 0) + (NLON - MARGIN)
    lam = 2.0 * math.pi * (column % NLON).astype(f32) / NLON
    waves = tide_ref[0:1] * jnp.cos(tide_ref[2:3] * lam + tide_ref[1:2])
    wide_lane = lax.broadcasted_iota(jnp.int32, (WIDE, TILE), 1)
    tide = []
    for moment in range(SUBSTEPS):
        pair = []
        for kind in range(2):
            low = 8 * moment + 4 * kind
            inside = (wide_lane >= low) & (wide_lane < low + 4)
            pair.append(jnp.sum(jnp.where(inside, waves, 0.0), axis=1, keepdims=True))
        tide.append(pair)

    for move in halo:
        move.wait_recv()

    has_lo = jnp.where(la > 0, 1.0, 0.0).astype(f32)
    has_hi = jnp.where(la < LATS - 1, 1.0, 0.0).astype(f32)
    for f in range(FIELDS):
        turned[16 * f : 16 * f + 8] = lo_recv[8 * f : 8 * f + 8] * has_lo
        turned[16 * f + 8 : 16 * f + 16] = hi_recv[8 * f : 8 * f + 8] * has_hi
    turned[16 * FIELDS :] = jnp.zeros((TILE - 16 * FIELDS, TILE), f32)
    middle = turned[...].T
    short = lax.broadcasted_iota(jnp.int32, (8, TILE), 1) % 16 < 8
    ends = [
        jnp.where(short, dg_recv[side, 0] * has_lo, dg_recv[side, 1] * has_hi) for side in range(2)
    ]
    edges = jnp.concatenate([ends[0], middle, ends[1]], axis=0)
    fields = []
    for f in range(FIELDS):
        core = jnp.concatenate([lf_recv[f], cores[f], rt_recv[f]], axis=0)
        edge = pltpu.roll(edges, TILE - (16 * f + 8), 1)
        fields.append(jnp.concatenate([core, edge], axis=1))

    h, u, v = stencil(fields, la, (cos, sec, coriolis, semi, diurnal), tide)
    h = h[MARGIN : MARGIN + TILE, 0:TILE]
    h_out[...] = h
    u_out[...] = u[MARGIN : MARGIN + TILE, 0:TILE]
    v_out[...] = v[MARGIN : MARGIN + TILE, 0:TILE]
    wet_h = wet_core * h

    sum_send[...] = jnp.broadcast_to(jnp.sum(wet_h, keepdims=True), (8, TILE))
    sum_recv[pl.ds(la, 1)] = sum_send[...][None]

    def send_sum(j, carry):
        pltpu.make_async_remote_copy(
            src_ref=sum_send, dst_ref=sum_recv.at[la], send_sem=many_send.at[0],
            recv_sem=many_recv.at[0], device_id=at(la + j, lo), device_id_type=MESH,
        ).start()
        return carry

    lax.fori_loop(1, LATS, send_sum, 0)

    def exchange(index, source, target):
        def send(j, carry):
            peer = (lo + j) % LONS
            pltpu.make_async_remote_copy(
                src_ref=source.at[peer], dst_ref=target.at[lo], send_sem=many_send.at[index],
                recv_sem=many_recv.at[index], device_id=at(la, peer), device_id_type=MESH,
            ).start()
            return carry

        target[pl.ds(lo, 1)] = source[pl.ds(lo, 1)]
        lax.fori_loop(1, LONS, send, 0)

    def take(sems, index, buffer, count):
        part = buffer.at[pl.ds(0, count)]
        pltpu.make_async_copy(part, part, sems.at[index]).wait()

    wet_h_t = wet_h.T
    wet_t = wet_core.T
    for s in range(LONS):
        a1s[s, 0:ROWS] = wet_h_t[ROWS * s : ROWS * s + ROWS]
        a1s[s, ROWS : 2 * ROWS] = wet_t[ROWS * s : ROWS * s + ROWS]
    exchange(1, a1s, a1r)
    for load in loads[1:4]:
        load.wait()
    take(many_recv, 1, a1r, LONS - 1)
    spectra = jnp.dot(first[...], a1r[...].reshape(256, TILE), precision=highest, preferred_element_type=f32)
    cos_t = twist[0]
    sin_t = twist[1]
    blocks = []
    for l in range(ROWS):
        parts = []
        for kind in range(2):
            start = 64 * (4 * kind + l)
            re = spectra[start : start + 32]
            im = spectra[start + 32 : start + 64]
            parts += [re * cos_t + im * sin_t, im * cos_t - re * sin_t]
        blocks.append(jnp.concatenate(parts, axis=1))
    twisted = jnp.concatenate(blocks, axis=0)
    full = lax.dot_general(
        second[...], twisted, (((1,), (1,)), ((), ())), precision=highest, preferred_element_type=f32
    )
    take(many_recv, 0, sum_recv, LATS - 1)
    band_sum = jnp.sum(sum_recv[...], axis=0)[0:1]
    kind_row = lax.broadcasted_iota(jnp.int32, (256, TILE), 0) % 8
    full = jnp.where(kind_row == 4, band_sum, full)
    a2s[...] = full.reshape(LONS, 8, TILE)
    exchange(2, a2s, a2r)
    loads[7].wait()
    loads[0].wait()
    take(many_recv, 2, a2r, LONS - 1)
    got = a2r[...].reshape(256, TILE)
    total = jnp.sum(jnp.where(kind_row == 4, got, 0.0), axis=0, keepdims=True)
    mean = total / jnp.sum(counts_ref[...].astype(f32), keepdims=True)
    fourier = (got - mean * pltpu.roll(got, 254, 0)).astype(bf16)
    placed = lax.dot_general(
        fourier, place[...], (((0,), (0,)), ((), ())), preferred_element_type=f32
    )
    waves_r = []
    for r in range(2):
        value = placed[0:32, 128 * r : 128 * r + 128]
        for l in range(1, ROWS):
            start = 256 * l + 128 * r
            value = value + placed[32 * l : 32 * l + 32, start : start + 128]
        waves_r.append(value)

    sub = lax.broadcasted_iota(jnp.int32, (16, TILE), 0) % 8
    for g in range(4):
        pair = jnp.concatenate([waves_r[0][8 * g : 8 * g + 8], waves_r[1][8 * g : 8 * g + 8]], axis=0)
        acc = jnp.zeros((16, NDEG), f32)
        for t in range(4):
            lhs = jnp.concatenate(
                [jnp.where(sub == 2 * t, pair, 0.0), jnp.where(sub == 2 * t + 1, pair, 0.0)], axis=1
            ).astype(bf16)
            rhs = jnp.concatenate([leg[8 * g + 2 * t], leg[8 * g + 2 * t + 1]], axis=1)
            acc = acc + lax.dot_general(
                lhs, rhs, (((1,), (1,)), ((), ())), preferred_element_type=f32
            )
        for d in range(LATS):
            cs[d, 16 * g : 16 * g + 16] = acc[:, 128 * d : 128 * d + 128]

    cr[pl.ds(la, 1)] = cs[pl.ds(la, 1)]

    def send_coefficients(j, carry):
        peer = (la + j) % LATS
        pltpu.make_async_remote_copy(
            src_ref=cs.at[peer], dst_ref=cr.at[la], send_sem=many_send.at[3],
            recv_sem=many_recv.at[3], device_id=at(peer, lo), device_id_type=MESH,
        ).start()
        return carry

    lax.fori_loop(1, LATS, send_coefficients, 0)
    love = love_ref[pl.ds(la, 1)]
    take(many_recv, 3, cr, LATS - 1)
    coefficients = jnp.sum(cr[...], axis=0)
    sg[pl.ds(la, 1)] = (coefficients * love).astype(bf16)[None]

    def send_scaled(j, carry):
        pltpu.make_async_remote_copy(
            src_ref=sg.at[la], dst_ref=sg.at[la], send_sem=many_send.at[4],
            recv_sem=many_recv.at[4], device_id=at(la + j, lo), device_id_type=MESH,
        ).start()
        return carry

    lax.fori_loop(1, LATS, send_scaled, 0)
    for load in loads[4:7] + loads[8:9]:
        load.wait()
    take(many_recv, 4, sg, LATS - 1)

    heads = []
    for g in range(4):
        lhs = jnp.concatenate([sg[d, 16 * g : 16 * g + 16] for d in range(LATS)], axis=1)
        acc = jnp.zeros((16, TILE), f32)
        for t in range(4):
            rhs = jnp.concatenate([leg[8 * g + 2 * t], leg[8 * g + 2 * t + 1]], axis=1)
            both = jnp.dot(lhs, rhs, preferred_element_type=f32)
            acc = jnp.where(sub == 2 * t, both[:, 0:TILE], acc)
            acc = jnp.where(sub == 2 * t + 1, both[:, TILE:], acc)
        if g == 0:
            weight = jnp.where((sub == 0) & (lo == 0), 1.0 / 64.0, 2.0 / 64.0)
            acc = acc * weight
        else:
            acc = acc * (2.0 / 64.0)
        heads.append(acc)
    both = jnp.concatenate(
        [
            jnp.concatenate([heads[g][0:8] for g in range(4)], axis=0),
            jnp.concatenate([heads[g][8:16] for g in range(4)], axis=0),
        ],
        axis=1,
    )
    empty = jnp.zeros((WAVES, 256), f32)
    stacked = jnp.concatenate(
        [
            jnp.concatenate([both if c == l else empty for c in range(ROWS)], axis=1)
            for l in range(ROWS)
        ],
        axis=0,
    )
    large = stacked.astype(bf16)
    small = (stacked - large.astype(f32)).astype(bf16)
    rows = lax.dot_general(
        spread[...], large, (((1,), (1,)), ((), ())), preferred_element_type=f32
    ) + lax.dot_general(spread[...], small, (((1,), (1,)), ((), ())), preferred_element_type=f32)
    for s in range(LONS):
        a3s[s] = rows[2 * s : 2 * s + 2]
    exchange(5, a3s, a3r)
    take(many_recv, 5, a3r, LONS - 1)
    waves_all = jnp.concatenate([a3r[s] for s in range(LONS)], axis=0)
    opened = jnp.dot(back[...], waves_all, precision=highest, preferred_element_type=f32)
    re = opened[0:TILE]
    im = opened[TILE:]
    cos_u = untwist[0]
    sin_u = untwist[1]
    untwisted = jnp.concatenate([re * cos_u - im * sin_u, re * sin_u + im * cos_u], axis=1)
    field = lax.dot_general(
        last[...], untwisted, (((1,), (1,)), ((), ())), precision=highest, preferred_element_type=f32
    )
    for s in range(LONS):
        a4s[s] = field[ROWS * s : ROWS * s + ROWS]
    exchange(6, a4s, a4r)
    take(many_recv, 6, a4r, LONS - 1)
    s_out[...] = jnp.concatenate([a4r[s] for s in range(LONS)], axis=0).T

    for move in halo:
        move.wait_send()
    take(many_send, 0, sum_recv, LATS - 1)
    take(many_send, 1, a1s, LONS - 1)
    take(many_send, 2, a2s, LONS - 1)
    take(many_send, 3, cs, LATS - 1)
    take(many_send, 4, sg, LATS - 1)
    take(many_send, 5, a3s, LONS - 1)
    take(many_send, 6, a4s, LONS - 1)


def shards(
    sea_level, east_velocity, north_velocity, depth, land_mask, wet_counts, loading_prev,
    tide_amp, tide_phase, legendre, love_factor,
):
    moments = jnp.arange(SUBSTEPS, dtype=f32)[:, None]
    phase = (moments * jnp.array(frequencies, f32)[None, :] + tide_phase[None, :]).reshape(32)
    amp = jnp.tile(tide_amp, SUBSTEPS)
    order = jnp.tile(jnp.array(orders, f32), SUBSTEPS)
    tide = jnp.pad(jnp.stack([amp, phase, order]), ((0, 5), (0, TILE - 32)))
    tables = make_tables()
    vmem = pl.BlockSpec(memory_space=pltpu.VMEM)
    hbm = pl.BlockSpec(memory_space=pl.ANY)
    shape = jax.ShapeDtypeStruct((TILE, TILE), f32)
    scratch = [pltpu.VMEM((WAVES, NDEG, TILE), bf16)]
    scratch += [pltpu.VMEM(x.shape, x.dtype) for x in tables]
    scratch += [
        pltpu.VMEM((48, TILE), f32), pltpu.VMEM((48, TILE), f32),
        pltpu.VMEM((48, TILE), f32), pltpu.VMEM((48, TILE), f32),
        pltpu.VMEM((FIELDS, 8, TILE), f32), pltpu.VMEM((FIELDS, 8, TILE), f32),
        pltpu.VMEM((FIELDS, 8, TILE), f32), pltpu.VMEM((FIELDS, 8, TILE), f32),
        pltpu.VMEM((2, 8, TILE), f32), pltpu.VMEM((2, 2, 8, TILE), f32),
        pltpu.VMEM((TILE, TILE), f32),
        pltpu.VMEM((8, TILE), f32), pltpu.VMEM((LATS, 8, TILE), f32),
        pltpu.VMEM((LONS, 8, TILE), f32), pltpu.VMEM((LONS, 8, TILE), f32),
        pltpu.VMEM((LONS, 8, TILE), f32), pltpu.VMEM((LONS, 8, TILE), f32),
        pltpu.VMEM((LATS, 64, TILE), f32), pltpu.VMEM((LATS, 64, TILE), f32),
        pltpu.VMEM((LATS, 64, TILE), bf16),
        pltpu.VMEM((LONS, 2, TILE), f32), pltpu.VMEM((LONS, 2, TILE), f32),
        pltpu.VMEM((LONS, ROWS, TILE), f32), pltpu.VMEM((LONS, ROWS, TILE), f32),
        pltpu.SemaphoreType.DMA((9,)),
        pltpu.SemaphoreType.DMA((8,)), pltpu.SemaphoreType.DMA((8,)),
        pltpu.SemaphoreType.DMA((7,)), pltpu.SemaphoreType.DMA((7,)),
    ]
    return pl.pallas_call(
        kernel,
        out_shape=(shape,) * 4,
        in_specs=[vmem] * 9 + [hbm] * 9,
        out_specs=(vmem,) * 4,
        scratch_shapes=scratch,
        compiler_params=pltpu.CompilerParams(
            collective_id=0, has_side_effects=True, vmem_limit_bytes=40 * 1024 * 1024
        ),
        name="tide",
    )(
        sea_level, east_velocity, north_velocity, depth, land_mask, loading_prev, tide, wet_counts,
        love_factor.reshape(LATS, NDEG // LATS), legendre, *[jnp.asarray(x) for x in tables],
    )


def solution(mesh):
    grid = P("lon", "lat")
    return jax.shard_map(
        shards,
        mesh=mesh,
        in_specs=(grid, grid, grid, grid, grid, P(), grid, P(), P(), P("lon", None, "lat"), P()),
        out_specs=(grid, grid, grid, grid),
        check_vma=False,
    )
```

```python
import functools
import math

import jax
import jax.numpy as jnp
import ml_dtypes
import numpy as np
from jax import lax
from jax.experimental import pallas as pl
from jax.experimental.pallas import tpu as pltpu
from jax.sharding import PartitionSpec as P

SUBSTEPS = 4
NLON = 4096
NLAT = 1024
NDEG = 1024
LONS = 32
LATS = 8
TILE = 128
WAVES = 32
ROWS = TILE // LONS
MARGIN = 8
WIDE = TILE + 2 * MARGIN
FIELDS = 6
SLOTS = 4
VMEM_BYTES = 56 * 1024 * 1024

lat_edge = 1.3089969
courant = 0.4
friction = 0.02
rotation = 0.2
frequencies = (0.1405, 0.1454, 0.1379, 0.1458, 0.0729, 0.0676, 0.0725, 0.0649)
orders = (2, 2, 2, 2, 1, 1, 1, 1)
highest = lax.Precision.HIGHEST
MESH = pl.DeviceIdType.MESH
f32 = jnp.float32
bf16 = jnp.bfloat16


def turn(product, period):
    angle = 2.0 * np.pi * (product % period) / period
    return np.cos(angle), np.sin(angle)


def split(table):
    high = table.astype(ml_dtypes.bfloat16)
    low = (table - high.astype(np.float64)).astype(ml_dtypes.bfloat16)
    return np.concatenate([high, high, low], axis=1)


def make_tables():
    band = np.arange(32)
    cell = np.arange(128)
    cos, sin = turn(np.outer(band, band), 32)
    first = np.zeros((ROWS, 2, 32, 32, ROWS))
    for row in range(ROWS):
        first[row, 0, :, :, row] = cos
        first[row, 1, :, :, row] = -sin
    first = first.reshape(256, 128)
    cos, sin = turn(np.outer(band, cell), 4096)
    extra = np.zeros((8, 128))
    extra[0, :32] = (np.arange(SUBSTEPS)[:, None] * np.array(frequencies)[None, :]).reshape(-1)
    extra[1, :32] = np.tile(np.array(orders), SUBSTEPS)
    twist = np.concatenate([cos, sin, extra])
    cos, sin = turn(np.outer(band, cell), 128)
    second = np.zeros((32, SLOTS, 2, 128))
    second[:, 0, 0] = cos / 64.0
    second[:, 0, 1] = sin / 64.0
    second[:, 1, 0] = -sin / 64.0
    second[:, 1, 1] = cos / 64.0
    second = second.reshape(128, 256)
    place = np.zeros((32, SLOTS, ROWS, 2, 128))
    for s in range(32):
        for row in range(ROWS):
            for r in range(2):
                place[s, r, row, r, ROWS * s + row] = 1.0
    spread = place[:, :2].reshape(64, 1024)
    place = place.reshape(128, 1024)
    cos, sin = turn(np.outer(cell, band), 128)
    back = np.zeros((2, 128, 32, 2))
    back[0, :, :, 0] = cos
    back[0, :, :, 1] = -sin
    back[1, :, :, 0] = sin
    back[1, :, :, 1] = cos
    back = back.reshape(256, 64)
    cos, sin = turn(np.outer(cell, band), 4096)
    untwist = np.stack([np.tile(cos, (1, ROWS)), np.tile(sin, (1, ROWS))])
    cos, sin = turn(np.outer(band, band), 32)
    last = np.zeros((32, ROWS, 2, ROWS, 32))
    for row in range(ROWS):
        last[:, row, 0, row, :] = cos
        last[:, row, 1, row, :] = -sin
    last = last.reshape(128, 256)
    plain = [x.astype(np.float32) for x in (twist, untwist)]
    exact = [x.astype(ml_dtypes.bfloat16) for x in (place, spread)]
    return [split(first), plain[0], split(second), exact[0], split(back), plain[1], split(last), exact[1]]


def halves(value, axis):
    high = value.astype(bf16)
    low = (value - high.astype(f32)).astype(bf16)
    return jnp.concatenate([high, low, high], axis=axis)


def stencil(fields, la, north_table, tide):
    h, u, v, depth, wet, loading = fields
    cos, sec, coriolis, semi, diurnal = north_table

    def up(x, axis):
        return pltpu.roll(x, x.shape[axis] - 1, axis)

    def down(x, axis):
        return pltpu.roll(x, 1, axis)

    for moment in range(SUBSTEPS):
        forcing = semi * tide[moment][0] + diurnal * tide[moment][1]
        flux_east = depth * u
        flux_north = depth * v * cos
        divergence = (
            (up(flux_east, 0) - down(flux_east, 0) + (up(flux_north, 1) - down(flux_north, 1)))
            * 0.5
            * sec
        )
        h = h - courant * divergence * wet
        pressure = h - forcing - loading
        slope_east = (up(pressure, 0) - down(pressure, 0)) * 0.5 * sec
        slope_north = (up(pressure, 1) - down(pressure, 1)) * 0.5
        u, v = (
            wet * ((1.0 - friction) * u + courant * (coriolis * v - slope_east)),
            wet * ((1.0 - friction) * v - courant * (coriolis * u + slope_north)),
        )
    return h, u, v


def across(lhs, rhs):
    return lax.dot_general(lhs, rhs, (((1,), (1,)), ((), ())), preferred_element_type=f32)


def kernel(
    sea_hbm, east_hbm, north_hbm, depth_hbm, mask_hbm, load_hbm, amp_hbm, phase_hbm, counts_hbm, love_hbm,
    leg_hbm, first_hbm, twist_hbm, second_hbm, place_hbm, back_hbm, untwist_hbm, last_hbm, spread_hbm,
    h_hbm, u_hbm, v_hbm, s_hbm,
    sea_ref, east_ref, north_ref, depth_ref, mask_ref, load_ref, amp_ref, phase_ref, counts_ref, love_ref,
    leg, first, twist, second, place, back, untwist, last, spread,
    up_send, dn_send, lo_recv, hi_recv, lf_send, rt_send, lf_recv, rt_recv, dg_send, dg_recv, turned,
    sum_send, sum_recv, a0s, a0r, a1s, a1r, aws, awr, a2s, a2r, lhs_ref, cs, cr, sg, acc_ref, a3s, a3r, a4s, a4r,
    h_out, u_out, v_out, s_out,
    local_sem, halo_send, halo_recv, many_send, many_recv, scaled_recv, store_sem,
):
    la = lax.axis_index("lat")
    lo = lax.axis_index("lon")

    def at(lat, lon):
        return {"lat": lat % LATS, "lon": lon % LONS}

    pairs = (
        (sea_hbm, sea_ref), (east_hbm, east_ref), (north_hbm, north_ref), (depth_hbm, depth_ref),
        (mask_hbm, mask_ref), (load_hbm, load_ref), (amp_hbm, amp_ref), (phase_hbm, phase_ref),
        (twist_hbm, twist), (first_hbm, first), (second_hbm, second), (place_hbm, place),
        (counts_hbm, counts_ref), (leg_hbm, leg), (love_hbm, love_ref), (spread_hbm, spread),
        (back_hbm, back), (untwist_hbm, untwist), (last_hbm, last),
    )
    loads = [
        pltpu.make_async_copy(src, dst, local_sem.at[i]) for i, (src, dst) in enumerate(pairs)
    ]
    for load in loads[0:6]:
        load.start()

    barrier = pltpu.get_barrier_semaphore()

    def greet_lon(j, carry):
        pl.semaphore_signal(barrier, inc=1, device_id=at(la, lo + j), device_id_type=MESH)
        return carry

    def greet_lat(j, carry):
        pl.semaphore_signal(barrier, inc=1, device_id=at(la + j, lo), device_id_type=MESH)
        return carry

    lax.fori_loop(1, LATS, greet_lat, 0)
    for dl in (1, LATS - 1):
        for dn in (1, LONS - 1):
            pl.semaphore_signal(barrier, inc=1, device_id=at(la + dl, lo + dn), device_id_type=MESH)
    lax.fori_loop(1, LONS, greet_lon, 0)
    for load in loads[6:]:
        load.start()
    for load in loads[0:6]:
        load.wait()

    wet_core = mask_ref[...].astype(f32)
    cores = [sea_ref[...], east_ref[...], north_ref[...], depth_ref[...], wet_core, load_ref[...]]
    lane = lax.broadcasted_iota(jnp.int32, (TILE, TILE), 1)
    packed = jnp.zeros((TILE, TILE), f32)
    for f in range(FIELDS):
        moved = pltpu.roll(cores[f], 16 * f + 8, 1)
        packed = jnp.where((lane >= 16 * f) & (lane < 16 * f + 16), moved, packed)
        lf_send[f] = cores[f][0:8]
        rt_send[f] = cores[f][TILE - 8 : TILE]
    dg_send[0] = packed[0:8]
    dg_send[1] = packed[TILE - 8 : TILE]
    packed_t = packed.T
    for f in range(FIELDS):
        up_send[8 * f : 8 * f + 8] = packed_t[16 * f : 16 * f + 8]
        dn_send[8 * f : 8 * f + 8] = packed_t[16 * f + 8 : 16 * f + 16]
    wet_t = wet_core.T
    for s in range(LONS):
        a0s[s] = wet_t[ROWS * s : ROWS * s + ROWS]

    slot = lax.broadcasted_iota(jnp.int32, (1, 2 * TILE), 1)
    row = la * TILE + jnp.where(slot < 192, slot, slot - 256)
    phi = -lat_edge + 2.0 * lat_edge * (row.astype(f32) + 0.5) / NLAT
    phi = jnp.clip(phi, -1.5, 1.5)
    cos = jnp.cos(phi)
    sec = 1.0 / cos
    coriolis = rotation * jnp.sin(phi)
    semi = cos * cos * (NLON / 64.0)
    diurnal = jnp.sin(2.0 * phi) * (NLON / 64.0)
    for load in loads[6:9]:
        load.wait()
    short_lane = lax.broadcasted_iota(jnp.int32, (1, TILE), 1)
    amp = jnp.zeros((1, TILE), f32)
    phase = jnp.zeros((1, TILE), f32)
    for c in range(8):
        hit = (short_lane % 8 == c) & (short_lane < 8 * SUBSTEPS)
        amp = jnp.where(hit, amp_ref[c], amp)
        phase = jnp.where(hit, phase_ref[c], phase)
    phase = phase + twist[64:65]
    column = lo * TILE + lax.broadcasted_iota(jnp.int32, (WIDE, TILE), 0) + (NLON - MARGIN)
    lam = 2.0 * math.pi * (column % NLON).astype(f32) / NLON
    waves = amp * jnp.cos(twist[65:66] * lam + phase)
    wide_lane = lax.broadcasted_iota(jnp.int32, (WIDE, TILE), 1)
    tide = []
    for moment in range(SUBSTEPS):
        pair = []
        for kind in range(2):
            low = 8 * moment + 4 * kind
            inside = (wide_lane >= low) & (wide_lane < low + 4)
            pair.append(jnp.sum(jnp.where(inside, waves, 0.0), axis=1, keepdims=True))
        tide.append(pair)

    pl.semaphore_wait(barrier, LONS - 1 + LATS - 1 + 4)

    moves = (
        (up_send, lo_recv, at(la + 1, lo)),
        (dn_send, hi_recv, at(la + LATS - 1, lo)),
        (dg_send.at[0], dg_recv.at[1, 0], at(la + 1, lo + LONS - 1)),
        (dg_send.at[0], dg_recv.at[1, 1], at(la + LATS - 1, lo + LONS - 1)),
        (dg_send.at[1], dg_recv.at[0, 0], at(la + 1, lo + 1)),
        (dg_send.at[1], dg_recv.at[0, 1], at(la + LATS - 1, lo + 1)),
        (lf_send, rt_recv, at(la, lo + LONS - 1)),
        (rt_send, lf_recv, at(la, lo + 1)),
    )
    halo = [
        pltpu.make_async_remote_copy(
            src_ref=src, dst_ref=dst, send_sem=halo_send.at[i], recv_sem=halo_recv.at[i],
            device_id=dev, device_id_type=MESH,
        )
        for i, (src, dst, dev) in enumerate(moves)
    ]
    for move in halo:
        move.start()

    def exchange(index, source, target):
        def one(peer):
            pltpu.make_async_remote_copy(
                src_ref=source.at[peer], dst_ref=target.at[lo], send_sem=many_send.at[index],
                recv_sem=many_recv.at[index], device_id=at(la, peer), device_id_type=MESH,
            ).start()

        for dx in (2, 1, 3, 0):

            def send(j, carry, dx=dx):
                one((lo // 8 + dx) % 4 * 8 + (lo + j) % 8)
                return carry

            lax.fori_loop(1 if dx == 0 else 0, 8, send, 0)
        target[pl.ds(lo, 1)] = source[pl.ds(lo, 1)]

    def take(sems, index, buffer, count):
        part = buffer.at[pl.ds(0, count)]
        pltpu.make_async_copy(part, part, sems.at[index]).wait()

    def rows_of(buffer):
        return jnp.concatenate([buffer[s] for s in range(LONS)], axis=0)

    exchange(7, a0s, a0r)

    for move in halo:
        move.wait_recv()

    has_lo = jnp.where(la > 0, 1.0, 0.0).astype(f32)
    has_hi = jnp.where(la < LATS - 1, 1.0, 0.0).astype(f32)
    for f in range(FIELDS):
        turned[16 * f : 16 * f + 8] = lo_recv[8 * f : 8 * f + 8] * has_lo
        turned[16 * f + 8 : 16 * f + 16] = hi_recv[8 * f : 8 * f + 8] * has_hi
    turned[16 * FIELDS :] = jnp.zeros((TILE - 16 * FIELDS, TILE), f32)
    middle = turned[...].T
    short = lax.broadcasted_iota(jnp.int32, (8, TILE), 1) % 16 < 8
    ends = [
        jnp.where(short, dg_recv[side, 0] * has_lo, dg_recv[side, 1] * has_hi) for side in range(2)
    ]
    edges = jnp.concatenate([ends[0], middle, ends[1]], axis=0)
    fields = []
    for f in range(FIELDS):
        core = jnp.concatenate([lf_recv[f], cores[f], rt_recv[f]], axis=0)
        edge = pltpu.roll(edges, TILE - (16 * f + 8), 1)
        fields.append(jnp.concatenate([core, edge], axis=1))

    h, u, v = stencil(fields, la, (cos, sec, coriolis, semi, diurnal), tide)
    h = h[MARGIN : MARGIN + TILE, 0:TILE]
    wet_h = wet_core * h
    wet_h_t = wet_h.T
    for s in range(LONS):
        a1s[s] = wet_h_t[ROWS * s : ROWS * s + ROWS]
    sum_send[...] = jnp.broadcast_to(jnp.sum(wet_h, keepdims=True), (1, TILE))
    sum_recv[pl.ds(la, 1)] = sum_send[...][None]

    def send_sum(j, carry):
        pltpu.make_async_remote_copy(
            src_ref=sum_send, dst_ref=sum_recv.at[la], send_sem=many_send.at[0],
            recv_sem=many_recv.at[0], device_id=at(la + j, lo), device_id_type=MESH,
        ).start()
        return carry

    lax.fori_loop(1, LATS, send_sum, 0)
    exchange(1, a1s, a1r)
    h_out[...] = h
    u_out[...] = u[MARGIN : MARGIN + TILE, 0:TILE]
    v_out[...] = v[MARGIN : MARGIN + TILE, 0:TILE]
    stores = [
        pltpu.make_async_copy(src, dst, store_sem.at[i])
        for i, (src, dst) in enumerate(
            ((h_out, h_hbm), (u_out, u_hbm), (v_out, v_hbm), (s_out, s_hbm))
        )
    ]
    for store in stores[0:3]:
        store.start()

    def analyse(spectra):
        cos_t = twist[0:32]
        sin_t = twist[32:64]
        blocks = []
        for l in range(ROWS):
            re = spectra[64 * l : 64 * l + 32]
            im = spectra[64 * l + 32 : 64 * l + 64]
            blocks.append(
                jnp.concatenate([re * cos_t + im * sin_t, im * cos_t - re * sin_t], axis=1)
            )
        return across(second[...], halves(jnp.concatenate(blocks, axis=0), 1))

    for load in loads[9:12]:
        load.wait()
    take(many_recv, 7, a0r, LONS - 1)
    mask_rows = rows_of(a0r).astype(bf16)
    full = analyse(
        jnp.dot(
            first[:, TILE:], jnp.concatenate([mask_rows, mask_rows], axis=0), preferred_element_type=f32
        )
    )
    for s in range(LONS):
        aws[s] = full[SLOTS * s : SLOTS * s + SLOTS]
    exchange(8, aws, awr)
    take(many_recv, 0, sum_recv, LATS - 1)
    band_sum = jnp.sum(sum_recv[...], axis=0)
    take(many_recv, 1, a1r, LONS - 1)
    full = analyse(jnp.dot(first[...], halves(rows_of(a1r), 0), preferred_element_type=f32))
    kind_row = lax.broadcasted_iota(jnp.int32, (TILE, TILE), 0) % SLOTS
    full = jnp.where(kind_row == 2, band_sum, full)
    for s in range(LONS):
        a2s[s] = full[SLOTS * s : SLOTS * s + SLOTS]
    exchange(2, a2s, a2r)
    for load in loads[12:15]:
        load.wait()
    count = jnp.sum(counts_ref[...].astype(f32), keepdims=True)
    take(many_recv, 8, awr, LONS - 1)
    got_mask = rows_of(awr)
    take(many_recv, 2, a2r, LONS - 1)
    got = rows_of(a2r)
    total = jnp.sum(jnp.where(kind_row == 2, got, 0.0), axis=0, keepdims=True)
    fourier = (got - (total / count) * got_mask).astype(bf16)
    placed = lax.dot_general(
        fourier, place[...], (((0,), (0,)), ((), ())), preferred_element_type=f32
    )
    waves_r = []
    for r in range(2):
        value = placed[0:32, 128 * r : 128 * r + 128]
        for l in range(1, ROWS):
            start = 256 * l + 128 * r
            value = value + placed[32 * l : 32 * l + 32, start : start + 128]
        waves_r.append(value)

    sub = lax.broadcasted_iota(jnp.int32, (16, TILE), 0) % 8
    for g in range(4):
        pair = jnp.concatenate([waves_r[0][8 * g : 8 * g + 8], waves_r[1][8 * g : 8 * g + 8]], axis=0)
        for j in range(8):
            lhs_ref[g, :, TILE * j : TILE * j + TILE] = jnp.where(sub == j, pair, 0.0).astype(bf16)

    def send_coefficients(peer):
        pltpu.make_async_remote_copy(
            src_ref=cs.at[peer], dst_ref=cr.at[la], send_sem=many_send.at[3],
            recv_sem=many_recv.at[3], device_id=at(peer, lo), device_id_type=MESH,
        ).start()

    def analysis(t, carry):
        y = (la // 2 + 2 + t) % 4
        start = pl.multiple_of(y * 256, 256)
        for g in range(4):
            rhs = jnp.concatenate([leg[8 * g + j, pl.ds(start, 256), :] for j in range(8)], axis=1)
            acc = across(lhs_ref[g], rhs)
            cs[2 * y, 16 * g : 16 * g + 16] = acc[:, 0:TILE]
            cs[2 * y + 1, 16 * g : 16 * g + 16] = acc[:, TILE:]
        send_coefficients(2 * y + 1 - la % 2)

        @pl.when(t != 2)
        def _():
            send_coefficients(2 * y + la % 2)

        return carry

    lax.fori_loop(0, 4, analysis, 0)
    cr[pl.ds(la, 1)] = cs[pl.ds(la, 1)]
    love = love_ref[pl.ds(la, 1)]
    take(many_recv, 3, cr, LATS - 1)
    coefficients = jnp.sum(cr[...], axis=0)
    sg[pl.ds(la, 1)] = (coefficients * love).astype(bf16)[None]

    def send_scaled(j, carry):
        peer = (la + LATS - j) % LATS
        pltpu.make_async_remote_copy(
            src_ref=sg.at[la], dst_ref=sg.at[la], send_sem=many_send.at[4],
            recv_sem=scaled_recv.at[la], device_id=at(peer, lo), device_id_type=MESH,
        ).start()
        return carry

    lax.fori_loop(1, LATS, send_scaled, 0)
    for load in loads[15:]:
        load.wait()

    def take_scaled(owner):
        part = sg.at[owner]
        pltpu.make_async_copy(part, part, scaled_recv.at[owner]).wait()

    def synthesis(t, carry):
        y = (la // 2 + t) % 4

        @pl.when(t != 0)
        def _():
            take_scaled(2 * y + la % 2)

        take_scaled(2 * y + 1 - la % 2)
        start = pl.multiple_of(y * 256, 256)
        left = sg[2 * y]
        right = sg[2 * y + 1]
        for g in range(4):
            lhs = jnp.concatenate([left[16 * g : 16 * g + 16], right[16 * g : 16 * g + 16]], axis=1)
            for k in range(4):
                rhs = jnp.concatenate(
                    [leg[8 * g + 2 * k + i, pl.ds(start, 256), :] for i in range(2)], axis=1
                )
                acc_ref[4 * g + k] += jnp.dot(lhs, rhs, preferred_element_type=f32)
        return carry

    acc_ref[...] = jnp.zeros((16, 16, 256), f32)
    lax.fori_loop(0, 4, synthesis, 0)
    heads = []
    for g in range(4):
        acc = jnp.zeros((16, TILE), f32)
        for k in range(4):
            acc = jnp.where(sub == 2 * k, acc_ref[4 * g + k, :, 0:TILE], acc)
            acc = jnp.where(sub == 2 * k + 1, acc_ref[4 * g + k, :, TILE:], acc)
        if g == 0:
            weight = jnp.where((sub == 0) & (lo == 0), 1.0 / 64.0, 2.0 / 64.0)
            acc = acc * weight
        else:
            acc = acc * (2.0 / 64.0)
        heads.append(acc)
    both = jnp.concatenate(
        [
            jnp.concatenate([heads[g][0:8] for g in range(4)], axis=0),
            jnp.concatenate([heads[g][8:16] for g in range(4)], axis=0),
        ],
        axis=1,
    )
    empty = jnp.zeros((WAVES, 256), f32)
    stacked = jnp.concatenate(
        [
            jnp.concatenate([both if c == l else empty for c in range(ROWS)], axis=1)
            for l in range(ROWS)
        ],
        axis=0,
    )
    large = stacked.astype(bf16)
    tiny = (stacked - large.astype(f32)).astype(bf16)
    rows = across(spread[...], large) + across(spread[...], tiny)
    for s in range(LONS):
        a3s[s] = rows[2 * s : 2 * s + 2]
    exchange(5, a3s, a3r)
    take(many_recv, 5, a3r, LONS - 1)

    opened = jnp.dot(back[...], halves(rows_of(a3r), 0), preferred_element_type=f32)
    re = opened[0:TILE]
    im = opened[TILE:]
    cos_u = untwist[0]
    sin_u = untwist[1]
    untwisted = jnp.concatenate([re * cos_u - im * sin_u, re * sin_u + im * cos_u], axis=1)
    field = across(last[...], halves(untwisted, 1))
    for s in range(LONS):
        a4s[s] = field[ROWS * s : ROWS * s + ROWS]
    exchange(6, a4s, a4r)
    take(many_recv, 6, a4r, LONS - 1)
    s_out[...] = rows_of(a4r).T
    stores[3].start()

    for move in halo:
        move.wait_send()
    take(many_send, 0, sum_recv, LATS - 1)
    take(many_send, 1, a1s, LONS - 1)
    take(many_send, 2, a2s, LONS - 1)
    take(many_send, 3, cs, LATS - 1)
    take(many_send, 4, sg, LATS - 1)
    take(many_send, 5, a3s, LONS - 1)
    take(many_send, 6, a4s, LONS - 1)
    take(many_send, 7, a0s, LONS - 1)
    take(many_send, 8, aws, LONS - 1)
    for store in stores:
        store.wait()


def deliver(*refs):
    for i in range(4):
        refs[i + 4][...] = refs[i][...]


def shards(
    sea_level, east_velocity, north_velocity, depth, land_mask, wet_counts, loading_prev,
    tide_amp, tide_phase, legendre, love_factor,
):
    tables = make_tables()
    hbm = pl.BlockSpec(memory_space=pltpu.HBM)
    vmem = pl.BlockSpec(memory_space=pltpu.VMEM)
    shape = jax.ShapeDtypeStruct((TILE, TILE), f32)
    tile = pltpu.VMEM((TILE, TILE), f32)
    slab = pltpu.VMEM((FIELDS, 8, TILE), f32)
    edge = pltpu.VMEM((48, TILE), f32)
    quad = pltpu.VMEM((LONS, SLOTS, TILE), f32)
    two = pltpu.VMEM((LONS, 2, TILE), f32)
    part = pltpu.VMEM((LATS, 64, TILE), f32)
    scratch = [tile, tile, tile, tile, pltpu.VMEM((TILE, TILE), jnp.int32), tile]
    scratch += [pltpu.SMEM((8,), f32), pltpu.SMEM((8,), f32)]
    scratch += [pltpu.VMEM((LATS, LONS), jnp.int32), pltpu.VMEM((LATS, TILE), f32)]
    scratch += [pltpu.VMEM((WAVES, NDEG, TILE), bf16)]
    scratch += [pltpu.VMEM(x.shape, x.dtype) for x in tables]
    scratch += [edge, edge, edge, edge, slab, slab, slab, slab]
    scratch += [pltpu.VMEM((2, 8, TILE), f32), pltpu.VMEM((2, 2, 8, TILE), f32), tile]
    scratch += [pltpu.VMEM((1, TILE), f32), pltpu.VMEM((LATS, 1, TILE), f32)]
    scratch += [quad] * 8
    scratch += [pltpu.VMEM((4, 16, 8 * TILE), bf16), part, part, pltpu.VMEM((LATS, 64, TILE), bf16)]
    scratch += [pltpu.VMEM((16, 16, 2 * TILE), f32), two, two, quad, quad]
    scratch += [tile] * 4
    scratch += [
        pltpu.SemaphoreType.DMA((19,)),
        pltpu.SemaphoreType.DMA((8,)), pltpu.SemaphoreType.DMA((8,)),
        pltpu.SemaphoreType.DMA((9,)), pltpu.SemaphoreType.DMA((9,)), pltpu.SemaphoreType.DMA((8,)),
        pltpu.SemaphoreType.DMA((4,)),
    ]
    results = pl.pallas_call(
        kernel,
        out_shape=(shape,) * 4,
        in_specs=[hbm] * 19,
        out_specs=(hbm,) * 4,
        scratch_shapes=scratch,
        compiler_params=pltpu.CompilerParams(
            collective_id=0, has_side_effects=True, vmem_limit_bytes=VMEM_BYTES
        ),
        name="tide",
    )(
        sea_level, east_velocity, north_velocity, depth, land_mask, loading_prev, tide_amp, tide_phase,
        wet_counts, love_factor.reshape(LATS, NDEG // LATS), legendre,
        *[jnp.asarray(x) for x in tables],
    )
    return pl.pallas_call(
        deliver,
        out_shape=(shape,) * 4,
        in_specs=[vmem] * 4,
        out_specs=(vmem,) * 4,
        name="deliver",
    )(*results)


def solution(mesh):
    grid = P("lon", "lat")
    return jax.shard_map(
        shards,
        mesh=mesh,
        in_specs=(grid, grid, grid, grid, grid, P(), grid, P(), P(), P("lon", None, "lat"), P()),
        out_specs=(grid, grid, grid, grid),
        check_vma=False,
    )
```

```python
import functools
import math

import jax
import jax.numpy as jnp
import ml_dtypes
import numpy as np
from jax import lax
from jax.experimental import pallas as pl
from jax.experimental.pallas import tpu as pltpu
from jax.sharding import PartitionSpec as P

SUBSTEPS = 4
NLON = 4096
NLAT = 1024
NDEG = 1024
LONS = 32
LATS = 8
TILE = 128
WAVES = 32
ROWS = TILE // LONS
MARGIN = 8
WIDE = TILE + 2 * MARGIN
FIELDS = 6
SLOTS = 4
QUARTER = NDEG // 4
VMEM_BYTES = 40 * 1024 * 1024

lat_edge = 1.3089969
courant = 0.4
friction = 0.02
rotation = 0.2
frequencies = (0.1405, 0.1454, 0.1379, 0.1458, 0.0729, 0.0676, 0.0725, 0.0649)
orders = (2, 2, 2, 2, 1, 1, 1, 1)
highest = lax.Precision.HIGHEST
MESH = pl.DeviceIdType.MESH
f32 = jnp.float32
bf16 = jnp.bfloat16


def turn(product, period):
    angle = 2.0 * np.pi * (product % period) / period
    return np.cos(angle), np.sin(angle)


def split(table):
    high = table.astype(ml_dtypes.bfloat16)
    low = (table - high.astype(np.float64)).astype(ml_dtypes.bfloat16)
    return np.concatenate([high, high, low], axis=1)


def make_tables():
    band = np.arange(32)
    cell = np.arange(128)
    cos, sin = turn(np.outer(band, band), 32)
    first = np.zeros((ROWS, 2, 32, 32, ROWS))
    for row in range(ROWS):
        first[row, 0, :, :, row] = cos
        first[row, 1, :, :, row] = -sin
    first = first.reshape(256, 128)
    cos, sin = turn(np.outer(band, cell), 4096)
    extra = np.zeros((8, 128))
    extra[0, :32] = (np.arange(SUBSTEPS)[:, None] * np.array(frequencies)[None, :]).reshape(-1)
    extra[1, :32] = np.tile(np.array(orders), SUBSTEPS)
    twist = np.concatenate([cos, sin, extra])
    cos, sin = turn(np.outer(band, cell), 128)
    second = np.zeros((32, SLOTS, 2, 128))
    second[:, 0, 0] = cos / 64.0
    second[:, 0, 1] = sin / 64.0
    second[:, 1, 0] = -sin / 64.0
    second[:, 1, 1] = cos / 64.0
    second = second.reshape(128, 256)
    place = np.zeros((32, SLOTS, ROWS, 2, 128))
    for s in range(32):
        for row in range(ROWS):
            for r in range(2):
                place[s, r, row, r, ROWS * s + row] = 1.0
    spread = place[:, :2].reshape(64, 1024)
    place = place.reshape(128, 1024)
    cos, sin = turn(np.outer(cell, band), 128)
    back = np.zeros((2, 128, 32, 2))
    back[0, :, :, 0] = cos
    back[0, :, :, 1] = -sin
    back[1, :, :, 0] = sin
    back[1, :, :, 1] = cos
    back = back.reshape(256, 64)
    cos, sin = turn(np.outer(cell, band), 4096)
    untwist = np.stack([np.tile(cos, (1, ROWS)), np.tile(sin, (1, ROWS))])
    cos, sin = turn(np.outer(band, band), 32)
    last = np.zeros((32, ROWS, 2, ROWS, 32))
    for row in range(ROWS):
        last[:, row, 0, row, :] = cos
        last[:, row, 1, row, :] = -sin
    last = last.reshape(128, 256)
    plain = [x.astype(np.float32) for x in (twist, untwist)]
    exact = [x.astype(ml_dtypes.bfloat16) for x in (place, spread)]
    return [split(first), plain[0], split(second), exact[0], split(back), plain[1], split(last), exact[1]]


def halves(value, axis):
    high = value.astype(bf16)
    low = (value - high.astype(f32)).astype(bf16)
    return jnp.concatenate([high, low, high], axis=axis)


def stencil(fields, la, north_table, tide):
    h, u, v, depth, wet, loading = fields
    cos, sec, coriolis, semi, diurnal = north_table

    def up(x, axis):
        return pltpu.roll(x, x.shape[axis] - 1, axis)

    def down(x, axis):
        return pltpu.roll(x, 1, axis)

    for moment in range(SUBSTEPS):
        forcing = semi * tide[moment][0] + diurnal * tide[moment][1]
        flux_east = depth * u
        flux_north = depth * v * cos
        divergence = (
            (up(flux_east, 0) - down(flux_east, 0) + (up(flux_north, 1) - down(flux_north, 1)))
            * 0.5
            * sec
        )
        h = h - courant * divergence * wet
        pressure = h - forcing - loading
        slope_east = (up(pressure, 0) - down(pressure, 0)) * 0.5 * sec
        slope_north = (up(pressure, 1) - down(pressure, 1)) * 0.5
        u, v = (
            wet * ((1.0 - friction) * u + courant * (coriolis * v - slope_east)),
            wet * ((1.0 - friction) * v - courant * (coriolis * u + slope_north)),
        )
    return h, u, v


def across(lhs, rhs):
    return lax.dot_general(lhs, rhs, (((1,), (1,)), ((), ())), preferred_element_type=f32)


def kernel(
    sea_hbm, east_hbm, north_hbm, depth_hbm, mask_hbm, load_hbm, amp_hbm, phase_hbm, counts_hbm, love_hbm,
    leg_hbm, first_hbm, twist_hbm, second_hbm, place_hbm, back_hbm, untwist_hbm, last_hbm, spread_hbm,
    h_out, u_out, v_out, s_out,
    sea_ref, east_ref, north_ref, depth_ref, mask_ref, load_ref, amp_ref, phase_ref, counts_ref, love_ref,
    leg, first, twist, second, place, back, untwist, last, spread,
    up_send, dn_send, lo_recv, hi_recv, lf_send, rt_send, lf_recv, rt_recv, dg_send, dg_recv, turned,
    sum_send, sum_recv, a0s, a0r, a1s, a1r, aws, awr, a2s, a2r, lhs_ref, cs, cr, cb, db, sg, acc_ref, a3s, a3r, a4s, a4r,
    local_sem, halo_send, halo_recv, many_send, many_recv, scaled_recv,
):
    la = lax.axis_index("lat")
    lo = lax.axis_index("lon")

    def at(lat, lon):
        return {"lat": lat % LATS, "lon": lon % LONS}

    pairs = (
        (sea_hbm, sea_ref), (east_hbm, east_ref), (north_hbm, north_ref), (depth_hbm, depth_ref),
        (mask_hbm, mask_ref), (load_hbm, load_ref), (amp_hbm, amp_ref), (phase_hbm, phase_ref),
        (twist_hbm, twist), (first_hbm, first), (second_hbm, second), (place_hbm, place),
        (counts_hbm, counts_ref), (leg_hbm, leg), (love_hbm, love_ref), (spread_hbm, spread),
        (back_hbm, back), (untwist_hbm, untwist), (last_hbm, last),
    )
    loads = [
        pltpu.make_async_copy(src, dst, local_sem.at[i]) for i, (src, dst) in enumerate(pairs)
    ]
    for load in loads[0:6]:
        load.start()

    barrier = pltpu.get_barrier_semaphore()

    def greet_lon(j, carry):
        pl.semaphore_signal(barrier, inc=1, device_id=at(la, lo + j), device_id_type=MESH)
        return carry

    def greet_lat(j, carry):
        pl.semaphore_signal(barrier, inc=1, device_id=at(la + j, lo), device_id_type=MESH)
        return carry

    lax.fori_loop(1, LATS, greet_lat, 0)
    for dl in (1, LATS - 1):
        for dn in (1, LONS - 1):
            pl.semaphore_signal(barrier, inc=1, device_id=at(la + dl, lo + dn), device_id_type=MESH)
    lax.fori_loop(1, LONS, greet_lon, 0)
    for load in loads[6:]:
        load.start()
    for load in loads[0:6]:
        load.wait()

    wet_core = mask_ref[...].astype(f32)
    cores = [sea_ref[...], east_ref[...], north_ref[...], depth_ref[...], wet_core, load_ref[...]]
    lane = lax.broadcasted_iota(jnp.int32, (TILE, TILE), 1)
    packed = jnp.zeros((TILE, TILE), f32)
    for f in range(FIELDS):
        moved = pltpu.roll(cores[f], 16 * f + 8, 1)
        packed = jnp.where((lane >= 16 * f) & (lane < 16 * f + 16), moved, packed)
        lf_send[f] = cores[f][0:8]
        rt_send[f] = cores[f][TILE - 8 : TILE]
    dg_send[0] = packed[0:8]
    dg_send[1] = packed[TILE - 8 : TILE]
    packed_t = packed.T
    for f in range(FIELDS):
        up_send[8 * f : 8 * f + 8] = packed_t[16 * f : 16 * f + 8]
        dn_send[8 * f : 8 * f + 8] = packed_t[16 * f + 8 : 16 * f + 16]
    wet_t = wet_core.T
    for s in range(LONS):
        a0s[s] = wet_t[ROWS * s : ROWS * s + ROWS]

    slot = lax.broadcasted_iota(jnp.int32, (1, 2 * TILE), 1)
    row = la * TILE + jnp.where(slot < 192, slot, slot - 256)
    phi = -lat_edge + 2.0 * lat_edge * (row.astype(f32) + 0.5) / NLAT
    phi = jnp.clip(phi, -1.5, 1.5)
    cos = jnp.cos(phi)
    sec = 1.0 / cos
    coriolis = rotation * jnp.sin(phi)
    semi = cos * cos * (NLON / 64.0)
    diurnal = jnp.sin(2.0 * phi) * (NLON / 64.0)
    for load in loads[6:9]:
        load.wait()
    short_lane = lax.broadcasted_iota(jnp.int32, (1, TILE), 1)
    amp = jnp.zeros((1, TILE), f32)
    phase = jnp.zeros((1, TILE), f32)
    for c in range(8):
        hit = (short_lane % 8 == c) & (short_lane < 8 * SUBSTEPS)
        amp = jnp.where(hit, amp_ref[c], amp)
        phase = jnp.where(hit, phase_ref[c], phase)
    phase = phase + twist[64:65]
    column = lo * TILE + lax.broadcasted_iota(jnp.int32, (WIDE, TILE), 0) + (NLON - MARGIN)
    lam = 2.0 * math.pi * (column % NLON).astype(f32) / NLON
    waves = amp * jnp.cos(twist[65:66] * lam + phase)
    wide_lane = lax.broadcasted_iota(jnp.int32, (WIDE, TILE), 1)
    tide = []
    for moment in range(SUBSTEPS):
        pair = []
        for kind in range(2):
            low = 8 * moment + 4 * kind
            inside = (wide_lane >= low) & (wide_lane < low + 4)
            pair.append(jnp.sum(jnp.where(inside, waves, 0.0), axis=1, keepdims=True))
        tide.append(pair)

    pl.semaphore_wait(barrier, LONS - 1 + LATS - 1 + 4)

    moves = (
        (dg_send.at[0], dg_recv.at[1, 0], at(la + 1, lo + LONS - 1)),
        (dg_send.at[0], dg_recv.at[1, 1], at(la + LATS - 1, lo + LONS - 1)),
        (dg_send.at[1], dg_recv.at[0, 0], at(la + 1, lo + 1)),
        (dg_send.at[1], dg_recv.at[0, 1], at(la + LATS - 1, lo + 1)),
        (up_send, lo_recv, at(la + 1, lo)),
        (dn_send, hi_recv, at(la + LATS - 1, lo)),
        (lf_send, rt_recv, at(la, lo + LONS - 1)),
        (rt_send, lf_recv, at(la, lo + 1)),
    )
    halo = [
        pltpu.make_async_remote_copy(
            src_ref=src, dst_ref=dst, send_sem=halo_send.at[i], recv_sem=halo_recv.at[i],
            device_id=dev, device_id_type=MESH,
        )
        for i, (src, dst, dev) in enumerate(moves)
    ]
    for move in halo:
        move.start()

    def exchange(index, source, target):
        def one(peer):
            pltpu.make_async_remote_copy(
                src_ref=source.at[peer], dst_ref=target.at[lo], send_sem=many_send.at[index],
                recv_sem=many_recv.at[index], device_id=at(la, peer), device_id_type=MESH,
            ).start()

        for dx in (2, 1, 3, 0):

            def send(j, carry, dx=dx):
                one((lo // 8 + dx) % 4 * 8 + (lo + j) % 8)
                return carry

            lax.fori_loop(1 if dx == 0 else 0, 8, send, 0)
        target[pl.ds(lo, 1)] = source[pl.ds(lo, 1)]

    def take(sems, index, buffer, count):
        part = buffer.at[pl.ds(0, count)]
        pltpu.make_async_copy(part, part, sems.at[index]).wait()

    def rows_of(buffer):
        return jnp.concatenate([buffer[s] for s in range(LONS)], axis=0)

    exchange(7, a0s, a0r)

    for move in halo:
        move.wait_recv()

    has_lo = jnp.where(la > 0, 1.0, 0.0).astype(f32)
    has_hi = jnp.where(la < LATS - 1, 1.0, 0.0).astype(f32)
    for f in range(FIELDS):
        turned[16 * f : 16 * f + 8] = lo_recv[8 * f : 8 * f + 8] * has_lo
        turned[16 * f + 8 : 16 * f + 16] = hi_recv[8 * f : 8 * f + 8] * has_hi
    turned[16 * FIELDS :] = jnp.zeros((TILE - 16 * FIELDS, TILE), f32)
    middle = turned[...].T
    short = lax.broadcasted_iota(jnp.int32, (8, TILE), 1) % 16 < 8
    ends = [
        jnp.where(short, dg_recv[side, 0] * has_lo, dg_recv[side, 1] * has_hi) for side in range(2)
    ]
    edges = jnp.concatenate([ends[0], middle, ends[1]], axis=0)
    fields = []
    for f in range(FIELDS):
        core = jnp.concatenate([lf_recv[f], cores[f], rt_recv[f]], axis=0)
        edge = pltpu.roll(edges, TILE - (16 * f + 8), 1)
        fields.append(jnp.concatenate([core, edge], axis=1))

    h, u, v = stencil(fields, la, (cos, sec, coriolis, semi, diurnal), tide)
    h = h[MARGIN : MARGIN + TILE, 0:TILE]
    wet_h = wet_core * h

    sum_send[...] = jnp.sum(wet_h, axis=0, keepdims=True)
    sum_recv[pl.ds(la, 1)] = sum_send[...][None]

    def send_sum(j, carry):
        pltpu.make_async_remote_copy(
            src_ref=sum_send, dst_ref=sum_recv.at[la], send_sem=many_send.at[0],
            recv_sem=many_recv.at[0], device_id=at(la + j, lo), device_id_type=MESH,
        ).start()
        return carry

    lax.fori_loop(1, LATS, send_sum, 0)
    wet_h_t = wet_h.T
    for s in range(LONS):
        a1s[s] = wet_h_t[ROWS * s : ROWS * s + ROWS]
    exchange(1, a1s, a1r)
    h_out[...] = h
    u_out[...] = u[MARGIN : MARGIN + TILE, 0:TILE]
    v_out[...] = v[MARGIN : MARGIN + TILE, 0:TILE]

    def analyse(spectra):
        cos_t = twist[0:32]
        sin_t = twist[32:64]
        blocks = []
        for l in range(ROWS):
            re = spectra[64 * l : 64 * l + 32]
            im = spectra[64 * l + 32 : 64 * l + 64]
            blocks.append(
                jnp.concatenate([re * cos_t + im * sin_t, im * cos_t - re * sin_t], axis=1)
            )
        return across(second[...], halves(jnp.concatenate(blocks, axis=0), 1))

    for load in loads[9:12]:
        load.wait()
    take(many_recv, 7, a0r, LONS - 1)
    mask_rows = rows_of(a0r).astype(bf16)
    full = analyse(
        jnp.dot(
            first[:, TILE:], jnp.concatenate([mask_rows, mask_rows], axis=0), preferred_element_type=f32
        )
    )
    for s in range(LONS):
        aws[s] = full[SLOTS * s : SLOTS * s + SLOTS]
    exchange(8, aws, awr)
    take(many_recv, 0, sum_recv, LATS - 1)
    band_sum = jnp.sum(sum_recv[...], axis=0)
    take(many_recv, 1, a1r, LONS - 1)
    full = analyse(jnp.dot(first[...], halves(rows_of(a1r), 0), preferred_element_type=f32))
    kind_row = lax.broadcasted_iota(jnp.int32, (TILE, TILE), 0) % SLOTS
    full = jnp.where(kind_row == 2, band_sum, full)
    for s in range(LONS):
        a2s[s] = full[SLOTS * s : SLOTS * s + SLOTS]
    exchange(2, a2s, a2r)
    for load in loads[12:15]:
        load.wait()
    count = jnp.sum(counts_ref[...].astype(f32), keepdims=True)
    take(many_recv, 8, awr, LONS - 1)
    got_mask = rows_of(awr)
    take(many_recv, 2, a2r, LONS - 1)
    got = rows_of(a2r)
    total = jnp.sum(jnp.where(kind_row == 2, got, 0.0), keepdims=True)
    fourier = (got - (total / count) * got_mask).astype(bf16)
    placed = lax.dot_general(
        fourier, place[...], (((0,), (0,)), ((), ())), preferred_element_type=f32
    )
    waves_r = []
    for r in range(2):
        value = placed[0:32, 128 * r : 128 * r + 128]
        for l in range(1, ROWS):
            start = 256 * l + 128 * r
            value = value + placed[32 * l : 32 * l + 32, start : start + 128]
        waves_r.append(value)

    sub = lax.broadcasted_iota(jnp.int32, (16, TILE), 0) % 8
    for g in range(4):
        pair = jnp.concatenate([waves_r[0][8 * g : 8 * g + 8], waves_r[1][8 * g : 8 * g + 8]], axis=0)
        for j in range(8):
            lhs_ref[g, :, TILE * j : TILE * j + TILE] = jnp.where(sub == j, pair, 0.0).astype(bf16)

    near = la % 2
    y_own = la // 2

    def y_at(t):
        return (y_own + 2 + t - t // 2 * (2 * t - 1)) % 4

    def analysis(t, carry):
        y = y_at(t)
        start = pl.multiple_of(y * QUARTER, QUARTER)
        for g in range(4):
            rhs = jnp.concatenate([leg[8 * g + j, pl.ds(start, QUARTER), :] for j in range(8)], axis=1)
            acc = across(lhs_ref[g], rhs)
            cs[y, 16 * g : 16 * g + 16] = acc
            cb[y, 16 * g : 16 * g + 16] = acc.astype(bf16)
        pltpu.make_async_remote_copy(
            src_ref=cb.at[y], dst_ref=db.at[y_own], send_sem=many_send.at[9],
            recv_sem=many_recv.at[9], device_id=at(2 * y + 1 - near, lo), device_id_type=MESH,
        ).start()

        @pl.when(t != 3)
        def _():
            pltpu.make_async_remote_copy(
                src_ref=cs.at[y], dst_ref=cr.at[y_own], send_sem=many_send.at[3],
                recv_sem=many_recv.at[3], device_id=at(2 * y + near, lo), device_id_type=MESH,
            ).start()

        return carry

    lax.fori_loop(0, 4, analysis, 0)
    cr[pl.ds(y_own, 1)] = cs[pl.ds(y_own, 1)]
    love = jnp.concatenate([love_ref[pl.ds(2 * y_own, 1)], love_ref[pl.ds(2 * y_own + 1, 1)]], axis=1)
    take(many_recv, 3, cr, 3)
    coefficients = jnp.sum(cr[...], axis=0)
    take(many_recv, 9, db, 4)
    coefficients = coefficients + jnp.sum(db[...].astype(f32), axis=0)
    sg[pl.ds(y_own, 1)] = (coefficients * love).astype(bf16)[None]

    def send_scaled(t, carry):
        pltpu.make_async_remote_copy(
            src_ref=sg.at[y_own], dst_ref=sg.at[y_own], send_sem=many_send.at[4],
            recv_sem=scaled_recv.at[y_own], device_id=at(2 * y_at(t) + near, lo), device_id_type=MESH,
        ).start()
        return carry

    lax.fori_loop(0, 3, send_scaled, 0)
    for load in loads[15:]:
        load.wait()

    def take_scaled(owner):
        part = sg.at[owner]
        pltpu.make_async_copy(part, part, scaled_recv.at[owner]).wait()

    def synthesis(t, carry):
        owner = y_at(3 - t)

        @pl.when(t != 0)
        def _():
            take_scaled(owner)

        start = pl.multiple_of(owner * QUARTER, QUARTER)
        scaled = sg[owner]
        for g in range(4):
            lhs = scaled[16 * g : 16 * g + 16]
            for k in range(4):
                rhs = jnp.concatenate(
                    [leg[8 * g + 2 * k + i, pl.ds(start, QUARTER), :] for i in range(2)], axis=1
                )
                acc_ref[4 * g + k] += jnp.dot(lhs, rhs, preferred_element_type=f32)
        return carry

    acc_ref[...] = jnp.zeros((16, 16, 256), f32)
    lax.fori_loop(0, 4, synthesis, 0)
    heads = []
    for g in range(4):
        acc = jnp.zeros((16, TILE), f32)
        for k in range(4):
            acc = jnp.where(sub == 2 * k, acc_ref[4 * g + k, :, 0:TILE], acc)
            acc = jnp.where(sub == 2 * k + 1, acc_ref[4 * g + k, :, TILE:], acc)
        if g == 0:
            weight = jnp.where((sub == 0) & (lo == 0), 1.0 / 64.0, 2.0 / 64.0)
            acc = acc * weight
        else:
            acc = acc * (2.0 / 64.0)
        heads.append(acc)
    both = jnp.concatenate(
        [
            jnp.concatenate([heads[g][0:8] for g in range(4)], axis=0),
            jnp.concatenate([heads[g][8:16] for g in range(4)], axis=0),
        ],
        axis=1,
    )
    empty = jnp.zeros((WAVES, 256), f32)
    stacked = jnp.concatenate(
        [
            jnp.concatenate([both if c == l else empty for c in range(ROWS)], axis=1)
            for l in range(ROWS)
        ],
        axis=0,
    )
    large = stacked.astype(bf16)
    tiny = (stacked - large.astype(f32)).astype(bf16)
    rows = across(spread[...], large) + across(spread[...], tiny)
    for s in range(LONS):
        a3s[s] = rows[2 * s : 2 * s + 2]
    exchange(5, a3s, a3r)
    take(many_recv, 5, a3r, LONS - 1)

    opened = jnp.dot(back[...], halves(rows_of(a3r), 0), preferred_element_type=f32)
    re = opened[0:TILE]
    im = opened[TILE:]
    cos_u = untwist[0]
    sin_u = untwist[1]
    untwisted = jnp.concatenate([re * cos_u - im * sin_u, re * sin_u + im * cos_u], axis=1)
    field = across(last[...], halves(untwisted, 1))
    for s in range(LONS):
        a4s[s] = field[ROWS * s : ROWS * s + ROWS]
    exchange(6, a4s, a4r)
    take(many_recv, 6, a4r, LONS - 1)
    s_out[...] = rows_of(a4r).T

    for move in halo:
        move.wait_send()
    take(many_send, 0, sum_recv, LATS - 1)
    take(many_send, 1, a1s, LONS - 1)
    take(many_send, 2, a2s, LONS - 1)
    take(many_send, 3, cs, 3)
    take(many_send, 9, cb, 4)
    take(many_send, 4, sg, 3)
    take(many_send, 5, a3s, LONS - 1)
    take(many_send, 6, a4s, LONS - 1)
    take(many_send, 7, a0s, LONS - 1)
    take(many_send, 8, aws, LONS - 1)


def deliver(*refs):
    sems = refs[-1]
    copies = [pltpu.make_async_copy(refs[i], refs[i + 4], sems.at[i]) for i in range(4)]
    for copy in copies:
        copy.start()
    for copy in copies:
        copy.wait()


def shards(
    sea_level, east_velocity, north_velocity, depth, land_mask, wet_counts, loading_prev,
    tide_amp, tide_phase, legendre, love_factor,
):
    tables = make_tables()
    hbm = pl.BlockSpec(memory_space=pltpu.HBM)
    vmem = pl.BlockSpec(memory_space=pltpu.VMEM)
    shape = jax.ShapeDtypeStruct((TILE, TILE), f32)
    tile = pltpu.VMEM((TILE, TILE), f32)
    slab = pltpu.VMEM((FIELDS, 8, TILE), f32)
    edge = pltpu.VMEM((48, TILE), f32)
    quad = pltpu.VMEM((LONS, SLOTS, TILE), f32)
    two = pltpu.VMEM((LONS, 2, TILE), f32)
    part = pltpu.VMEM((4, 64, QUARTER), f32)
    rough = pltpu.VMEM((4, 64, QUARTER), bf16)
    scratch = [tile, tile, tile, tile, pltpu.VMEM((TILE, TILE), jnp.int32), tile]
    scratch += [pltpu.SMEM((8,), f32), pltpu.SMEM((8,), f32)]
    scratch += [pltpu.VMEM((LATS, LONS), jnp.int32), pltpu.VMEM((LATS, TILE), f32)]
    scratch += [pltpu.VMEM((WAVES, NDEG, TILE), bf16)]
    scratch += [pltpu.VMEM(x.shape, x.dtype) for x in tables]
    scratch += [edge, edge, edge, edge, slab, slab, slab, slab]
    scratch += [pltpu.VMEM((2, 8, TILE), f32), pltpu.VMEM((2, 2, 8, TILE), f32), tile]
    scratch += [pltpu.VMEM((1, TILE), f32), pltpu.VMEM((LATS, 1, TILE), f32)]
    scratch += [quad] * 8
    scratch += [pltpu.VMEM((4, 16, 8 * TILE), bf16), part, part, rough, rough, rough]
    scratch += [pltpu.VMEM((16, 16, 2 * TILE), f32), two, two, quad, quad]
    scratch += [
        pltpu.SemaphoreType.DMA((19,)),
        pltpu.SemaphoreType.DMA((8,)), pltpu.SemaphoreType.DMA((8,)),
        pltpu.SemaphoreType.DMA((10,)), pltpu.SemaphoreType.DMA((10,)), pltpu.SemaphoreType.DMA((4,)),
    ]
    results = pl.pallas_call(
        kernel,
        out_shape=(shape,) * 4,
        in_specs=[hbm] * 19,
        out_specs=(vmem,) * 4,
        scratch_shapes=scratch,
        compiler_params=pltpu.CompilerParams(
            collective_id=0, has_side_effects=True, vmem_limit_bytes=VMEM_BYTES
        ),
        name="tide",
    )(
        *[
            pltpu.with_memory_space_constraint(x, pltpu.HBM)
            for x in (
                sea_level, east_velocity, north_velocity, depth, land_mask, loading_prev, tide_amp,
                tide_phase, wet_counts, love_factor.reshape(LATS, NDEG // LATS), legendre,
                *[jnp.asarray(x) for x in tables],
            )
        ]
    )
    return pl.pallas_call(
        deliver,
        out_shape=(shape,) * 4,
        in_specs=[pl.BlockSpec(memory_space=pl.ANY)] * 4,
        out_specs=(hbm,) * 4,
        scratch_shapes=[pltpu.SemaphoreType.DMA((4,))],
        compiler_params=pltpu.CompilerParams(vmem_limit_bytes=1024 * 1024),
        name="deliver",
    )(*results)


def solution(mesh):
    grid = P("lon", "lat")
    return jax.shard_map(
        shards,
        mesh=mesh,
        in_specs=(grid, grid, grid, grid, grid, P(), grid, P(), P(), P("lon", None, "lat"), P()),
        out_specs=(grid, grid, grid, grid),
        check_vma=False,
    )
```

```python
import functools
import math

import jax
import jax.numpy as jnp
import ml_dtypes
import numpy as np
from jax import lax
from jax.experimental import pallas as pl
from jax.experimental.pallas import tpu as pltpu
from jax.sharding import PartitionSpec as P

SUBSTEPS = 4
NLON = 4096
NLAT = 1024
NDEG = 1024
LONS = 32
LATS = 8
TILE = 128
WAVES = 32
ROWS = TILE // LONS
MARGIN = 8
WIDE = TILE + 2 * MARGIN
FIELDS = 6
SLOTS = 4
QUARTER = NDEG // 4
VMEM_BYTES = 40 * 1024 * 1024

lat_edge = 1.3089969
courant = 0.4
friction = 0.02
rotation = 0.2
frequencies = (0.1405, 0.1454, 0.1379, 0.1458, 0.0729, 0.0676, 0.0725, 0.0649)
orders = (2, 2, 2, 2, 1, 1, 1, 1)
highest = lax.Precision.HIGHEST
MESH = pl.DeviceIdType.MESH
f32 = jnp.float32
bf16 = jnp.bfloat16


def turn(product, period):
    angle = 2.0 * np.pi * (product % period) / period
    return np.cos(angle), np.sin(angle)


def split(table):
    high = table.astype(ml_dtypes.bfloat16)
    low = (table - high.astype(np.float64)).astype(ml_dtypes.bfloat16)
    return np.concatenate([high, high, low], axis=1)


def make_tables():
    band = np.arange(32)
    cell = np.arange(128)
    cos, sin = turn(np.outer(band, band), 32)
    first = np.zeros((ROWS, 2, 32, 32, ROWS))
    for row in range(ROWS):
        first[row, 0, :, :, row] = cos
        first[row, 1, :, :, row] = -sin
    first = first.reshape(256, 128)
    cos, sin = turn(np.outer(band, cell), 4096)
    extra = np.zeros((8, 128))
    extra[0, :32] = (np.arange(SUBSTEPS)[:, None] * np.array(frequencies)[None, :]).reshape(-1)
    extra[1, :32] = np.tile(np.array(orders), SUBSTEPS)
    twist = np.concatenate([cos, sin, extra])
    cos, sin = turn(np.outer(band, cell), 128)
    second = np.zeros((32, SLOTS, 2, 128))
    second[:, 0, 0] = cos / 64.0
    second[:, 0, 1] = sin / 64.0
    second[:, 1, 0] = -sin / 64.0
    second[:, 1, 1] = cos / 64.0
    second = second.reshape(128, 256)
    place = np.zeros((32, SLOTS, ROWS, 2, 128))
    for s in range(32):
        for row in range(ROWS):
            for r in range(2):
                place[s, r, row, r, ROWS * s + row] = 1.0
    spread = place[:, :2].reshape(8, 4, 2, 1024).transpose(0, 2, 1, 3).reshape(64, 1024)
    place = place.reshape(128, 1024)
    cos, sin = turn(np.outer(cell, band), 128)
    back = np.zeros((4, 2, 128, 32, 2, 4))
    for quad in range(4):
        back[quad, 0, :, :, 0, quad] = cos
        back[quad, 0, :, :, 1, quad] = -sin
        back[quad, 1, :, :, 0, quad] = sin
        back[quad, 1, :, :, 1, quad] = cos
    back = back.reshape(1024, 256)
    cos, sin = turn(np.outer(cell, band), 4096)
    untwist = np.stack([np.tile(cos, (1, ROWS)), np.tile(sin, (1, ROWS))])
    cos, sin = turn(np.outer(band, band), 32)
    last = np.zeros((32, ROWS, 2, ROWS, 32))
    for row in range(ROWS):
        last[:, row, 0, row, :] = cos
        last[:, row, 1, row, :] = -sin
    last = last.reshape(128, 256)
    plain = [x.astype(np.float32) for x in (twist, untwist)]
    exact = [x.astype(ml_dtypes.bfloat16) for x in (place, spread)]
    return [split(first), plain[0], split(second), exact[0], split(back)[:, 256:], plain[1], split(last), exact[1]]


def halves(value, axis):
    high = value.astype(bf16)
    low = (value - high.astype(f32)).astype(bf16)
    return jnp.concatenate([high, low, high], axis=axis)


def stencil(fields, la, north_table, tide):
    h, u, v, depth, wet, loading = fields
    cos, sec, coriolis, semi, diurnal = north_table

    def up(x, axis):
        return pltpu.roll(x, x.shape[axis] - 1, axis)

    def down(x, axis):
        return pltpu.roll(x, 1, axis)

    for moment in range(SUBSTEPS):
        forcing = semi * tide[moment][0] + diurnal * tide[moment][1]
        flux_east = depth * u
        flux_north = depth * v * cos
        divergence = (
            (up(flux_east, 0) - down(flux_east, 0) + (up(flux_north, 1) - down(flux_north, 1)))
            * 0.5
            * sec
        )
        h = h - courant * divergence * wet
        pressure = h - forcing - loading
        slope_east = (up(pressure, 0) - down(pressure, 0)) * 0.5 * sec
        slope_north = (up(pressure, 1) - down(pressure, 1)) * 0.5
        u, v = (
            wet * ((1.0 - friction) * u + courant * (coriolis * v - slope_east)),
            wet * ((1.0 - friction) * v - courant * (coriolis * u + slope_north)),
        )
    return h, u, v


def across(lhs, rhs):
    return lax.dot_general(lhs, rhs, (((1,), (1,)), ((), ())), preferred_element_type=f32)


def kernel(
    sea_hbm, east_hbm, north_hbm, depth_hbm, mask_hbm, load_hbm, amp_hbm, phase_hbm, counts_hbm, love_hbm,
    leg_hbm, first_hbm, twist_hbm, second_hbm, place_hbm, back_hbm, untwist_hbm, last_hbm, spread_hbm,
    h_out, u_out, v_out, s_out,
    sea_ref, east_ref, north_ref, depth_ref, mask_ref, load_ref, amp_ref, phase_ref, counts_ref, love_ref,
    leg, first, twist, second, place, back, untwist, last, spread,
    up_send, dn_send, lo_recv, hi_recv, lf_send, rt_send, lf_recv, rt_recv, dg_send, dg_recv, turned,
    sum_send, sum_recv, a0s, a0r, a1s, a1r, aws, awr, a2s, a2r, lhs_ref, cs, cr, cb, db, sg, acc_ref, a3s, a3r, a4s, a4r,
    local_sem, halo_send, halo_recv, many_send, many_recv, scaled_recv,
):
    la = lax.axis_index("lat")
    lo = lax.axis_index("lon")

    def at(lat, lon):
        return {"lat": lat % LATS, "lon": lon % LONS}

    pairs = (
        (sea_hbm, sea_ref), (east_hbm, east_ref), (north_hbm, north_ref), (depth_hbm, depth_ref),
        (mask_hbm, mask_ref), (load_hbm, load_ref), (amp_hbm, amp_ref), (phase_hbm, phase_ref),
        (twist_hbm, twist), (first_hbm, first), (second_hbm, second), (place_hbm, place),
        (counts_hbm, counts_ref), (leg_hbm, leg), (love_hbm, love_ref), (spread_hbm, spread),
        (back_hbm, back), (untwist_hbm, untwist), (last_hbm, last),
    )
    loads = [
        pltpu.make_async_copy(src, dst, local_sem.at[i]) for i, (src, dst) in enumerate(pairs)
    ]
    for load in loads[0:6]:
        load.start()

    barrier = pltpu.get_barrier_semaphore()

    def greet_lon(j, carry):
        pl.semaphore_signal(barrier, inc=1, device_id=at(la, lo + j), device_id_type=MESH)
        return carry

    def greet_lat(j, carry):
        pl.semaphore_signal(barrier, inc=1, device_id=at(la + j, lo), device_id_type=MESH)
        return carry

    lax.fori_loop(1, LATS, greet_lat, 0)
    for dl in (1, LATS - 1):
        for dn in (1, LONS - 1):
            pl.semaphore_signal(barrier, inc=1, device_id=at(la + dl, lo + dn), device_id_type=MESH)
    lax.fori_loop(1, LONS, greet_lon, 0)
    for load in loads[6:]:
        load.start()
    for load in loads[0:6]:
        load.wait()

    wet_core = mask_ref[...].astype(f32)
    cores = [sea_ref[...], east_ref[...], north_ref[...], depth_ref[...], wet_core, load_ref[...]]
    lane = lax.broadcasted_iota(jnp.int32, (TILE, TILE), 1)
    packed = jnp.zeros((TILE, TILE), f32)
    for f in range(FIELDS):
        moved = pltpu.roll(cores[f], 16 * f + 8, 1)
        packed = jnp.where((lane >= 16 * f) & (lane < 16 * f + 16), moved, packed)
        lf_send[f] = cores[f][0:8]
        rt_send[f] = cores[f][TILE - 8 : TILE]
    dg_send[0] = packed[0:8]
    dg_send[1] = packed[TILE - 8 : TILE]
    packed_t = packed.T
    for f in range(FIELDS):
        up_send[8 * f : 8 * f + 8] = packed_t[16 * f : 16 * f + 8]
        dn_send[8 * f : 8 * f + 8] = packed_t[16 * f + 8 : 16 * f + 16]
    wet_t = wet_core.T
    for s in range(LONS):
        a0s[s] = wet_t[ROWS * s : ROWS * s + ROWS]

    slot = lax.broadcasted_iota(jnp.int32, (1, 2 * TILE), 1)
    row = la * TILE + jnp.where(slot < 192, slot, slot - 256)
    phi = -lat_edge + 2.0 * lat_edge * (row.astype(f32) + 0.5) / NLAT
    phi = jnp.clip(phi, -1.5, 1.5)
    cos = jnp.cos(phi)
    sec = 1.0 / cos
    coriolis = rotation * jnp.sin(phi)
    semi = cos * cos * (NLON / 64.0)
    diurnal = jnp.sin(2.0 * phi) * (NLON / 64.0)
    for load in loads[6:9]:
        load.wait()
    short_lane = lax.broadcasted_iota(jnp.int32, (1, TILE), 1)
    amp = jnp.zeros((1, TILE), f32)
    phase = jnp.zeros((1, TILE), f32)
    for c in range(8):
        hit = (short_lane % 8 == c) & (short_lane < 8 * SUBSTEPS)
        amp = jnp.where(hit, amp_ref[c], amp)
        phase = jnp.where(hit, phase_ref[c], phase)
    phase = phase + twist[64:65]
    column = lo * TILE + lax.broadcasted_iota(jnp.int32, (WIDE, TILE), 0) + (NLON - MARGIN)
    lam = 2.0 * math.pi * (column % NLON).astype(f32) / NLON
    waves = amp * jnp.cos(twist[65:66] * lam + phase)
    wide_lane = lax.broadcasted_iota(jnp.int32, (WIDE, TILE), 1)
    tide = []
    for moment in range(SUBSTEPS):
        pair = []
        for kind in range(2):
            low = 8 * moment + 4 * kind
            inside = (wide_lane >= low) & (wide_lane < low + 4)
            pair.append(jnp.sum(jnp.where(inside, waves, 0.0), axis=1, keepdims=True))
        tide.append(pair)

    pl.semaphore_wait(barrier, LONS - 1 + LATS - 1 + 4)

    moves = (
        (dg_send.at[0], dg_recv.at[1, 0], at(la + 1, lo + LONS - 1)),
        (dg_send.at[0], dg_recv.at[1, 1], at(la + LATS - 1, lo + LONS - 1)),
        (dg_send.at[1], dg_recv.at[0, 0], at(la + 1, lo + 1)),
        (dg_send.at[1], dg_recv.at[0, 1], at(la + LATS - 1, lo + 1)),
        (up_send, lo_recv, at(la + 1, lo)),
        (dn_send, hi_recv, at(la + LATS - 1, lo)),
        (lf_send, rt_recv, at(la, lo + LONS - 1)),
        (rt_send, lf_recv, at(la, lo + 1)),
    )
    halo = [
        pltpu.make_async_remote_copy(
            src_ref=src, dst_ref=dst, send_sem=halo_send.at[i], recv_sem=halo_recv.at[i],
            device_id=dev, device_id_type=MESH,
        )
        for i, (src, dst, dev) in enumerate(moves)
    ]
    for move in halo:
        move.start()

    def exchange(index, source, target):
        def one(peer):
            pltpu.make_async_remote_copy(
                src_ref=source.at[peer], dst_ref=target.at[lo], send_sem=many_send.at[index],
                recv_sem=many_recv.at[index], device_id=at(la, peer), device_id_type=MESH,
            ).start()

        for dx in (2, 1, 3, 0):

            def send(j, carry, dx=dx):
                one((lo // 8 + dx) % 4 * 8 + (lo + j) % 8)
                return carry

            lax.fori_loop(1 if dx == 0 else 0, 8, send, 0)
        target[pl.ds(lo, 1)] = source[pl.ds(lo, 1)]

    def take(sems, index, buffer, count):
        part = buffer.at[pl.ds(0, count)]
        pltpu.make_async_copy(part, part, sems.at[index]).wait()

    def rows_of(buffer):
        return jnp.concatenate([buffer[s] for s in range(LONS)], axis=0)

    for move in halo[6:]:
        move.wait_recv()
    exchange(7, a0s, a0r)
    for move in halo[0:6]:
        move.wait_recv()

    has_lo = jnp.where(la > 0, 1.0, 0.0).astype(f32)
    has_hi = jnp.where(la < LATS - 1, 1.0, 0.0).astype(f32)
    for f in range(FIELDS):
        turned[16 * f : 16 * f + 8] = lo_recv[8 * f : 8 * f + 8] * has_lo
        turned[16 * f + 8 : 16 * f + 16] = hi_recv[8 * f : 8 * f + 8] * has_hi
    turned[16 * FIELDS :] = jnp.zeros((TILE - 16 * FIELDS, TILE), f32)
    middle = turned[...].T
    short = lax.broadcasted_iota(jnp.int32, (8, TILE), 1) % 16 < 8
    ends = [
        jnp.where(short, dg_recv[side, 0] * has_lo, dg_recv[side, 1] * has_hi) for side in range(2)
    ]
    edges = jnp.concatenate([ends[0], middle, ends[1]], axis=0)
    fields = []
    for f in range(FIELDS):
        core = jnp.concatenate([lf_recv[f], cores[f], rt_recv[f]], axis=0)
        edge = pltpu.roll(edges, TILE - (16 * f + 8), 1)
        fields.append(jnp.concatenate([core, edge], axis=1))

    h, u, v = stencil(fields, la, (cos, sec, coriolis, semi, diurnal), tide)
    h = h[MARGIN : MARGIN + TILE, 0:TILE]
    wet_h = wet_core * h

    sum_send[...] = jnp.sum(wet_h, axis=0, keepdims=True)
    sum_recv[pl.ds(la, 1)] = sum_send[...][None]

    def send_sum(j, carry):
        pltpu.make_async_remote_copy(
            src_ref=sum_send, dst_ref=sum_recv.at[la], send_sem=many_send.at[0],
            recv_sem=many_recv.at[0], device_id=at(la + j, lo), device_id_type=MESH,
        ).start()
        return carry

    lax.fori_loop(1, LATS, send_sum, 0)
    wet_h_t = wet_h.T
    for s in range(LONS):
        a1s[s] = wet_h_t[ROWS * s : ROWS * s + ROWS]
    exchange(1, a1s, a1r)
    h_out[...] = h
    u_out[...] = u[MARGIN : MARGIN + TILE, 0:TILE]
    v_out[...] = v[MARGIN : MARGIN + TILE, 0:TILE]

    def analyse(spectra):
        cos_t = twist[0:32]
        sin_t = twist[32:64]
        blocks = []
        for l in range(ROWS):
            re = spectra[64 * l : 64 * l + 32]
            im = spectra[64 * l + 32 : 64 * l + 64]
            blocks.append(
                jnp.concatenate([re * cos_t + im * sin_t, im * cos_t - re * sin_t], axis=1)
            )
        return across(second[...], halves(jnp.concatenate(blocks, axis=0), 1))

    for load in loads[9:12]:
        load.wait()
    take(many_recv, 7, a0r, LONS - 1)
    mask_rows = rows_of(a0r).astype(bf16)
    full = analyse(
        jnp.dot(
            first[:, TILE:], jnp.concatenate([mask_rows, mask_rows], axis=0), preferred_element_type=f32
        )
    )
    for s in range(LONS):
        aws[s] = full[SLOTS * s : SLOTS * s + SLOTS]
    exchange(8, aws, awr)
    take(many_recv, 0, sum_recv, LATS - 1)
    band_sum = jnp.sum(sum_recv[...], axis=0)
    take(many_recv, 1, a1r, LONS - 1)
    full = analyse(jnp.dot(first[...], halves(rows_of(a1r), 0), preferred_element_type=f32))
    kind_row = lax.broadcasted_iota(jnp.int32, (TILE, TILE), 0) % SLOTS
    full = jnp.where(kind_row == 2, band_sum, full)
    for s in range(LONS):
        a2s[s] = full[SLOTS * s : SLOTS * s + SLOTS]
    exchange(2, a2s, a2r)
    for load in loads[12:15]:
        load.wait()
    count = jnp.sum(counts_ref[...].astype(f32), keepdims=True)
    take(many_recv, 8, awr, LONS - 1)
    got_mask = rows_of(awr)
    take(many_recv, 2, a2r, LONS - 1)
    got = rows_of(a2r)
    total = jnp.sum(jnp.where(kind_row == 2, got, 0.0), keepdims=True)
    fourier = (got - (total / count) * got_mask).astype(bf16)
    placed = lax.dot_general(
        fourier, place[...], (((0,), (0,)), ((), ())), preferred_element_type=f32
    )
    waves_r = []
    for r in range(2):
        value = placed[0:32, 128 * r : 128 * r + 128]
        for l in range(1, ROWS):
            start = 256 * l + 128 * r
            value = value + placed[32 * l : 32 * l + 32, start : start + 128]
        waves_r.append(value)

    sub = lax.broadcasted_iota(jnp.int32, (16, TILE), 0) % 8
    for g in range(4):
        pair = jnp.concatenate([waves_r[0][8 * g : 8 * g + 8], waves_r[1][8 * g : 8 * g + 8]], axis=0)
        for j in range(8):
            lhs_ref[g, :, TILE * j : TILE * j + TILE] = jnp.where(sub == j, pair, 0.0).astype(bf16)

    near = la % 2
    y_own = la // 2

    def y_at(t):
        return (y_own + 2 + t - t // 2 * (2 * t - 1)) % 4

    def analysis(t, carry):
        y = y_at(t)
        start = pl.multiple_of(y * QUARTER, QUARTER)
        for g in range(4):
            rhs = jnp.concatenate([leg[8 * g + j, pl.ds(start, QUARTER), :] for j in range(8)], axis=1)
            acc = across(lhs_ref[g], rhs)
            cs[y, 16 * g : 16 * g + 16] = acc
            cb[y, 16 * g : 16 * g + 16] = acc.astype(bf16)
        pltpu.make_async_remote_copy(
            src_ref=cb.at[y], dst_ref=db.at[y_own], send_sem=many_send.at[9],
            recv_sem=many_recv.at[9], device_id=at(2 * y + 1 - near, lo), device_id_type=MESH,
        ).start()

        @pl.when(t != 3)
        def _():
            pltpu.make_async_remote_copy(
                src_ref=cs.at[y], dst_ref=cr.at[y_own], send_sem=many_send.at[3],
                recv_sem=many_recv.at[3], device_id=at(2 * y + near, lo), device_id_type=MESH,
            ).start()

        return carry

    lax.fori_loop(0, 4, analysis, 0)
    cr[pl.ds(y_own, 1)] = cs[pl.ds(y_own, 1)]
    love = jnp.concatenate([love_ref[pl.ds(2 * y_own, 1)], love_ref[pl.ds(2 * y_own + 1, 1)]], axis=1)
    take(many_recv, 3, cr, 3)
    coefficients = jnp.sum(cr[...], axis=0)
    take(many_recv, 9, db, 4)
    coefficients = coefficients + jnp.sum(db[...].astype(f32), axis=0)
    sg[pl.ds(y_own, 1)] = (coefficients * love).astype(bf16)[None]

    def send_scaled(t, carry):
        pltpu.make_async_remote_copy(
            src_ref=sg.at[y_own], dst_ref=sg.at[y_own], send_sem=many_send.at[4],
            recv_sem=scaled_recv.at[y_own], device_id=at(2 * y_at(t) + near, lo), device_id_type=MESH,
        ).start()
        return carry

    lax.fori_loop(0, 3, send_scaled, 0)
    for load in loads[15:]:
        load.wait()

    def take_scaled(owner):
        part = sg.at[owner]
        pltpu.make_async_copy(part, part, scaled_recv.at[owner]).wait()

    def synthesis(t, carry):
        owner = y_at(3 - t)

        @pl.when(t != 0)
        def _():
            take_scaled(owner)

        start = pl.multiple_of(owner * QUARTER, QUARTER)
        scaled = sg[owner]
        for g in range(4):
            lhs = scaled[16 * g : 16 * g + 16]
            for k in range(4):
                rhs = jnp.concatenate(
                    [leg[8 * g + 2 * k + i, pl.ds(start, QUARTER), :] for i in range(2)], axis=1
                )
                acc_ref[4 * g + k] += jnp.dot(lhs, rhs, preferred_element_type=f32)
        return carry

    acc_ref[...] = jnp.zeros((16, 16, 256), f32)
    lax.fori_loop(0, 4, synthesis, 0)
    heads = []
    for g in range(4):
        acc = jnp.zeros((16, TILE), f32)
        for k in range(4):
            acc = jnp.where(sub == 2 * k, acc_ref[4 * g + k, :, 0:TILE], acc)
            acc = jnp.where(sub == 2 * k + 1, acc_ref[4 * g + k, :, TILE:], acc)
        if g == 0:
            weight = jnp.where((sub == 0) & (lo == 0), 1.0 / 64.0, 2.0 / 64.0)
            acc = acc * weight
        else:
            acc = acc * (2.0 / 64.0)
        heads.append(acc)
    both = jnp.concatenate(
        [
            jnp.concatenate([heads[g][0:8] for g in range(4)], axis=0),
            jnp.concatenate([heads[g][8:16] for g in range(4)], axis=0),
        ],
        axis=1,
    )
    empty = jnp.zeros((WAVES, 256), f32)
    stacked = jnp.concatenate(
        [
            jnp.concatenate([both if c == l else empty for c in range(ROWS)], axis=1)
            for l in range(ROWS)
        ],
        axis=0,
    )
    rows = across(spread[...], stacked.astype(bf16))
    a3s[...] = rows.astype(bf16).reshape(8, 8, TILE)

    def send_rows(peer):
        pltpu.make_async_remote_copy(
            src_ref=a3s.at[peer % 8], dst_ref=a3r.at[lo], send_sem=many_send.at[5],
            recv_sem=many_recv.at[5], device_id=at(la, peer), device_id_type=MESH,
        ).start()

    for dx in (2, 1, 3, 0):

        def send_block(j, carry, dx=dx):
            send_rows((lo // 8 + dx) % 4 * 8 + (lo + j) % 8)
            return carry

        lax.fori_loop(1 if dx == 0 else 0, 8, send_block, 0)
    a3r[pl.ds(lo, 1)] = a3s[pl.ds(lo % 8, 1)]
    take(many_recv, 5, a3r, LONS - 1)

    every = a3r[...].reshape(256, TILE)
    opened = jnp.dot(back[...], jnp.concatenate([every, every], axis=0), preferred_element_type=f32)
    cos_u = untwist[0]
    sin_u = untwist[1]
    mine = last[pl.ds(pl.multiple_of(lo // 8 * 32, 32), 32), :]
    for quad in range(4):
        re = opened[256 * quad : 256 * quad + TILE]
        im = opened[256 * quad + TILE : 256 * quad + 256]
        untwisted = jnp.concatenate([re * cos_u - im * sin_u, re * sin_u + im * cos_u], axis=1)
        field = across(mine, halves(untwisted, 1))
        for e in range(8):
            a4s[e, 4 * quad : 4 * quad + 4] = field[4 * e : 4 * e + 4]

    def send_field(j, carry):
        e = (lo + j) % 8
        pltpu.make_async_remote_copy(
            src_ref=a4s.at[e], dst_ref=a4r.at[lo % 8], send_sem=many_send.at[6],
            recv_sem=many_recv.at[6], device_id=at(la, lo // 8 * 8 + e), device_id_type=MESH,
        ).start()
        return carry

    lax.fori_loop(1, 8, send_field, 0)
    a4r[pl.ds(lo % 8, 1)] = a4s[pl.ds(lo % 8, 1)]
    take(many_recv, 6, a4r, 7)
    s_out[...] = a4r[...].reshape(TILE, TILE).T

    for move in halo:
        move.wait_send()
    take(many_send, 0, sum_recv, LATS - 1)
    take(many_send, 1, a1s, LONS - 1)
    take(many_send, 2, a2s, LONS - 1)
    take(many_send, 3, cs, 3)
    take(many_send, 9, cb, 4)
    take(many_send, 4, sg, 3)
    take(many_send, 5, a3r, LONS - 1)
    take(many_send, 6, a4s, 7)
    take(many_send, 7, a0s, LONS - 1)
    take(many_send, 8, aws, LONS - 1)


def deliver(*refs):
    sems = refs[-1]
    copies = [pltpu.make_async_copy(refs[i], refs[i + 4], sems.at[i]) for i in range(4)]
    for copy in copies:
        copy.start()
    for copy in copies:
        copy.wait()


def shards(
    sea_level, east_velocity, north_velocity, depth, land_mask, wet_counts, loading_prev,
    tide_amp, tide_phase, legendre, love_factor,
):
    tables = make_tables()
    hbm = pl.BlockSpec(memory_space=pltpu.HBM)
    vmem = pl.BlockSpec(memory_space=pltpu.VMEM)
    shape = jax.ShapeDtypeStruct((TILE, TILE), f32)
    tile = pltpu.VMEM((TILE, TILE), f32)
    slab = pltpu.VMEM((FIELDS, 8, TILE), f32)
    edge = pltpu.VMEM((48, TILE), f32)
    quad = pltpu.VMEM((LONS, SLOTS, TILE), f32)
    part = pltpu.VMEM((4, 64, QUARTER), f32)
    rough = pltpu.VMEM((4, 64, QUARTER), bf16)
    scratch = [tile, tile, tile, tile, pltpu.VMEM((TILE, TILE), jnp.int32), tile]
    scratch += [pltpu.SMEM((8,), f32), pltpu.SMEM((8,), f32)]
    scratch += [pltpu.VMEM((LATS, LONS), jnp.int32), pltpu.VMEM((LATS, TILE), f32)]
    scratch += [pltpu.VMEM((WAVES, NDEG, TILE), bf16)]
    scratch += [pltpu.VMEM(x.shape, x.dtype) for x in tables]
    scratch += [edge, edge, edge, edge, slab, slab, slab, slab]
    scratch += [pltpu.VMEM((2, 8, TILE), f32), pltpu.VMEM((2, 2, 8, TILE), f32), tile]
    scratch += [pltpu.VMEM((1, TILE), f32), pltpu.VMEM((LATS, 1, TILE), f32)]
    scratch += [quad] * 8
    scratch += [pltpu.VMEM((4, 16, 8 * TILE), bf16), part, part, rough, rough, rough]
    scratch += [pltpu.VMEM((16, 16, 2 * TILE), f32), pltpu.VMEM((8, 8, TILE), bf16)]
    scratch += [pltpu.VMEM((LONS, 8, TILE), bf16)] + [pltpu.VMEM((8, 16, TILE), f32)] * 2
    scratch += [
        pltpu.SemaphoreType.DMA((19,)),
        pltpu.SemaphoreType.DMA((8,)), pltpu.SemaphoreType.DMA((8,)),
        pltpu.SemaphoreType.DMA((10,)), pltpu.SemaphoreType.DMA((10,)), pltpu.SemaphoreType.DMA((4,)),
    ]
    results = pl.pallas_call(
        kernel,
        out_shape=(shape,) * 4,
        in_specs=[hbm] * 19,
        out_specs=(vmem,) * 4,
        scratch_shapes=scratch,
        compiler_params=pltpu.CompilerParams(
            collective_id=0, has_side_effects=True, vmem_limit_bytes=VMEM_BYTES
        ),
        name="tide",
    )(
        *[
            pltpu.with_memory_space_constraint(x, pltpu.HBM)
            for x in (
                sea_level, east_velocity, north_velocity, depth, land_mask, loading_prev, tide_amp,
                tide_phase, wet_counts, love_factor.reshape(LATS, NDEG // LATS), legendre,
                *[jnp.asarray(x) for x in tables],
            )
        ]
    )
    return pl.pallas_call(
        deliver,
        out_shape=(shape,) * 4,
        in_specs=[pl.BlockSpec(memory_space=pl.ANY)] * 4,
        out_specs=(hbm,) * 4,
        scratch_shapes=[pltpu.SemaphoreType.DMA((4,))],
        compiler_params=pltpu.CompilerParams(vmem_limit_bytes=1024 * 1024),
        name="deliver",
    )(*results)


def solution(mesh):
    grid = P("lon", "lat")
    return jax.shard_map(
        shards,
        mesh=mesh,
        in_specs=(grid, grid, grid, grid, grid, P(), grid, P(), P(), P("lon", None, "lat"), P()),
        out_specs=(grid, grid, grid, grid),
        check_vma=False,
    )
```

```python
import functools
import math

import jax
import jax.numpy as jnp
import ml_dtypes
import numpy as np
from jax import lax
from jax.experimental import pallas as pl
from jax.experimental.pallas import tpu as pltpu
from jax.sharding import PartitionSpec as P

SUBSTEPS = 4
NLON = 4096
NLAT = 1024
NDEG = 1024
LONS = 32
LATS = 8
TILE = 128
WAVES = 32
ROWS = TILE // LONS
MARGIN = 8
WIDE = TILE + 2 * MARGIN
FIELDS = 6
SLOTS = 4
QUARTER = NDEG // 4
VMEM_BYTES = 40 * 1024 * 1024

lat_edge = 1.3089969
courant = 0.4
friction = 0.02
rotation = 0.2
frequencies = (0.1405, 0.1454, 0.1379, 0.1458, 0.0729, 0.0676, 0.0725, 0.0649)
orders = (2, 2, 2, 2, 1, 1, 1, 1)
highest = lax.Precision.HIGHEST
MESH = pl.DeviceIdType.MESH
f32 = jnp.float32
bf16 = jnp.bfloat16


def turn(product, period):
    angle = 2.0 * np.pi * (product % period) / period
    return np.cos(angle), np.sin(angle)


def split(table):
    high = table.astype(ml_dtypes.bfloat16)
    low = (table - high.astype(np.float64)).astype(ml_dtypes.bfloat16)
    return np.concatenate([high, high, low], axis=1)


def make_tables():
    band = np.arange(32)
    cell = np.arange(128)
    cos, sin = turn(np.outer(band, band), 32)
    first = np.zeros((ROWS, 2, 32, 32, ROWS))
    for row in range(ROWS):
        first[row, 0, :, :, row] = cos
        first[row, 1, :, :, row] = -sin
    first = first.reshape(256, 128)
    cos, sin = turn(np.outer(band, cell), 4096)
    extra = np.zeros((8, 128))
    extra[0, :32] = (np.arange(SUBSTEPS)[:, None] * np.array(frequencies)[None, :]).reshape(-1)
    extra[1, :32] = np.tile(np.array(orders), SUBSTEPS)
    twist = np.concatenate([cos, sin, extra])
    cos, sin = turn(np.outer(band, cell), 128)
    second = np.zeros((32, SLOTS, 2, 128))
    second[:, 0, 0] = cos / 64.0
    second[:, 0, 1] = sin / 64.0
    second[:, 1, 0] = -sin / 64.0
    second[:, 1, 1] = cos / 64.0
    second = second.reshape(128, 256)
    place = np.zeros((32, SLOTS, ROWS, 2, 128))
    for s in range(32):
        for row in range(ROWS):
            for r in range(2):
                place[s, r, row, r, ROWS * s + row] = 1.0
    spread = place[:, :2].reshape(8, 4, 2, 1024).transpose(0, 2, 1, 3).reshape(64, 1024)
    place = place.reshape(128, 1024)
    cos, sin = turn(np.outer(cell, band), 128)
    back = np.zeros((4, 2, 128, 32, 2, 4))
    for quad in range(4):
        back[quad, 0, :, :, 0, quad] = cos
        back[quad, 0, :, :, 1, quad] = -sin
        back[quad, 1, :, :, 0, quad] = sin
        back[quad, 1, :, :, 1, quad] = cos
    back = back.reshape(1024, 256)
    cos, sin = turn(np.outer(cell, band), 4096)
    untwist = np.stack([np.tile(cos, (1, ROWS)), np.tile(sin, (1, ROWS))])
    cos, sin = turn(np.outer(band, band), 32)
    last = np.zeros((32, ROWS, 2, ROWS, 32))
    for row in range(ROWS):
        last[:, row, 0, row, :] = cos
        last[:, row, 1, row, :] = -sin
    last = last.reshape(128, 256)
    plain = [x.astype(np.float32) for x in (twist, untwist)]
    exact = [x.astype(ml_dtypes.bfloat16) for x in (place, spread)]
    return [split(first), plain[0], split(second), exact[0], split(back)[:, 256:], plain[1], split(last), exact[1]]


def halves(value, axis):
    high = value.astype(bf16)
    low = (value - high.astype(f32)).astype(bf16)
    return jnp.concatenate([high, low, high], axis=axis)


def stencil(fields, la, north_table, tide):
    h, u, v, depth, wet, loading = fields
    cos, sec, coriolis, semi, diurnal = north_table

    def up(x, axis):
        return pltpu.roll(x, x.shape[axis] - 1, axis)

    def down(x, axis):
        return pltpu.roll(x, 1, axis)

    for moment in range(SUBSTEPS):
        forcing = semi * tide[moment][0] + diurnal * tide[moment][1]
        flux_east = depth * u
        flux_north = depth * v * cos
        divergence = (
            (up(flux_east, 0) - down(flux_east, 0) + (up(flux_north, 1) - down(flux_north, 1)))
            * 0.5
            * sec
        )
        h = h - courant * divergence * wet
        pressure = h - forcing - loading
        slope_east = (up(pressure, 0) - down(pressure, 0)) * 0.5 * sec
        slope_north = (up(pressure, 1) - down(pressure, 1)) * 0.5
        u, v = (
            wet * ((1.0 - friction) * u + courant * (coriolis * v - slope_east)),
            wet * ((1.0 - friction) * v - courant * (coriolis * u + slope_north)),
        )
    return h, u, v


def across(lhs, rhs):
    return lax.dot_general(lhs, rhs, (((1,), (1,)), ((), ())), preferred_element_type=f32)


def kernel(
    sea_hbm, east_hbm, north_hbm, depth_hbm, mask_hbm, load_hbm, amp_hbm, phase_hbm, counts_hbm, love_hbm,
    leg_hbm, first_hbm, twist_hbm, second_hbm, place_hbm, back_hbm, untwist_hbm, last_hbm, spread_hbm,
    h_out, u_out, v_out, s_out,
    sea_ref, east_ref, north_ref, depth_ref, mask_ref, load_ref, amp_ref, phase_ref, counts_ref, love_ref,
    leg, first, twist, second, place, back, untwist, last, spread,
    up_send, dn_send, lo_recv, hi_recv, lf_send, rt_send, lf_recv, rt_recv, dg_send, dg_recv, turned,
    sum_send, sum_recv, a0s, a0r, a1s, a1r, aws, awr, a2s, a2r, lhs_ref, cs, cr, cb, db, sg, acc_ref, a3s, a3r, a4s, a4r,
    local_sem, halo_send, halo_recv, many_send, many_recv, scaled_recv,
):
    la = lax.axis_index("lat")
    lo = lax.axis_index("lon")

    def at(lat, lon):
        return {"lat": lat % LATS, "lon": lon % LONS}

    pairs = (
        (sea_hbm, sea_ref), (east_hbm, east_ref), (north_hbm, north_ref), (depth_hbm, depth_ref),
        (mask_hbm, mask_ref), (load_hbm, load_ref), (amp_hbm, amp_ref), (phase_hbm, phase_ref),
        (twist_hbm, twist), (first_hbm, first), (second_hbm, second), (place_hbm, place),
        (counts_hbm, counts_ref), (leg_hbm, leg), (love_hbm, love_ref), (spread_hbm, spread),
        (back_hbm, back), (untwist_hbm, untwist), (last_hbm, last),
    )
    loads = [
        pltpu.make_async_copy(src, dst, local_sem.at[i]) for i, (src, dst) in enumerate(pairs)
    ]
    barrier = pltpu.get_barrier_semaphore()

    def greet_lon(j, carry):
        pl.semaphore_signal(barrier, inc=1, device_id=at(la, lo + j), device_id_type=MESH)
        return carry

    def greet_lat(j, carry):
        pl.semaphore_signal(barrier, inc=1, device_id=at(la + j, lo), device_id_type=MESH)
        return carry

    lax.fori_loop(1, LATS, greet_lat, 0)
    for dl in (1, LATS - 1):
        for dn in (1, LONS - 1):
            pl.semaphore_signal(barrier, inc=1, device_id=at(la + dl, lo + dn), device_id_type=MESH)
    for load in loads[0:6]:
        load.start()
    lax.fori_loop(1, LONS, greet_lon, 0)
    for load in loads[6:]:
        load.start()
    for load in loads[0:6]:
        load.wait()

    wet_core = mask_ref[...].astype(f32)
    cores = [sea_ref[...], east_ref[...], north_ref[...], depth_ref[...], wet_core, load_ref[...]]
    lane = lax.broadcasted_iota(jnp.int32, (TILE, TILE), 1)
    packed = jnp.zeros((TILE, TILE), f32)
    for f in range(FIELDS):
        moved = pltpu.roll(cores[f], 16 * f + 8, 1)
        packed = jnp.where((lane >= 16 * f) & (lane < 16 * f + 16), moved, packed)
        lf_send[f] = cores[f][0:8]
        rt_send[f] = cores[f][TILE - 8 : TILE]
    dg_send[0] = packed[0:8]
    dg_send[1] = packed[TILE - 8 : TILE]
    packed_t = packed.T
    for f in range(FIELDS):
        up_send[8 * f : 8 * f + 8] = packed_t[16 * f : 16 * f + 8]
        dn_send[8 * f : 8 * f + 8] = packed_t[16 * f + 8 : 16 * f + 16]
    wet_t = wet_core.T
    for s in range(LONS):
        a0s[s] = wet_t[ROWS * s : ROWS * s + ROWS]

    slot = lax.broadcasted_iota(jnp.int32, (1, 2 * TILE), 1)
    row = la * TILE + jnp.where(slot < 192, slot, slot - 256)
    phi = -lat_edge + 2.0 * lat_edge * (row.astype(f32) + 0.5) / NLAT
    phi = jnp.clip(phi, -1.5, 1.5)
    cos = jnp.cos(phi)
    sec = 1.0 / cos
    coriolis = rotation * jnp.sin(phi)
    semi = cos * cos * (NLON / 64.0)
    diurnal = jnp.sin(2.0 * phi) * (NLON / 64.0)
    for load in loads[6:9]:
        load.wait()
    short_lane = lax.broadcasted_iota(jnp.int32, (1, TILE), 1)
    amp = jnp.zeros((1, TILE), f32)
    phase = jnp.zeros((1, TILE), f32)
    for c in range(8):
        hit = (short_lane % 8 == c) & (short_lane < 8 * SUBSTEPS)
        amp = jnp.where(hit, amp_ref[c], amp)
        phase = jnp.where(hit, phase_ref[c], phase)
    phase = phase + twist[64:65]
    column = lo * TILE + lax.broadcasted_iota(jnp.int32, (WIDE, TILE), 0) + (NLON - MARGIN)
    lam = 2.0 * math.pi * (column % NLON).astype(f32) / NLON
    waves = amp * jnp.cos(twist[65:66] * lam + phase)
    wide_lane = lax.broadcasted_iota(jnp.int32, (WIDE, TILE), 1)
    tide = []
    for moment in range(SUBSTEPS):
        pair = []
        for kind in range(2):
            low = 8 * moment + 4 * kind
            inside = (wide_lane >= low) & (wide_lane < low + 4)
            pair.append(jnp.sum(jnp.where(inside, waves, 0.0), axis=1, keepdims=True))
        tide.append(pair)

    pl.semaphore_wait(barrier, LONS - 1 + LATS - 1 + 4)

    moves = (
        (dg_send.at[0], dg_recv.at[1, 0], at(la + 1, lo + LONS - 1)),
        (dg_send.at[0], dg_recv.at[1, 1], at(la + LATS - 1, lo + LONS - 1)),
        (dg_send.at[1], dg_recv.at[0, 0], at(la + 1, lo + 1)),
        (dg_send.at[1], dg_recv.at[0, 1], at(la + LATS - 1, lo + 1)),
        (up_send, lo_recv, at(la + 1, lo)),
        (dn_send, hi_recv, at(la + LATS - 1, lo)),
        (lf_send, rt_recv, at(la, lo + LONS - 1)),
        (rt_send, lf_recv, at(la, lo + 1)),
    )
    halo = [
        pltpu.make_async_remote_copy(
            src_ref=src, dst_ref=dst, send_sem=halo_send.at[i], recv_sem=halo_recv.at[i],
            device_id=dev, device_id_type=MESH,
        )
        for i, (src, dst, dev) in enumerate(moves)
    ]
    for move in halo:
        move.start()

    def exchange(index, source, target):
        def one(peer):
            pltpu.make_async_remote_copy(
                src_ref=source.at[peer], dst_ref=target.at[lo], send_sem=many_send.at[index],
                recv_sem=many_recv.at[index], device_id=at(la, peer), device_id_type=MESH,
            ).start()

        for dx in (2, 1, 3, 0):

            def send(j, carry, dx=dx):
                one((lo // 8 + dx) % 4 * 8 + (lo + j) % 8)
                return carry

            lax.fori_loop(1 if dx == 0 else 0, 8, send, 0)
        target[pl.ds(lo, 1)] = source[pl.ds(lo, 1)]

    def take(sems, index, buffer, count):
        part = buffer.at[pl.ds(0, count)]
        pltpu.make_async_copy(part, part, sems.at[index]).wait()

    def rows_of(buffer):
        return jnp.concatenate([buffer[s] for s in range(LONS)], axis=0)

    for move in halo[6:]:
        move.wait_recv()
    exchange(7, a0s, a0r)
    for move in halo[0:6]:
        move.wait_recv()

    has_lo = jnp.where(la > 0, 1.0, 0.0).astype(f32)
    has_hi = jnp.where(la < LATS - 1, 1.0, 0.0).astype(f32)
    for f in range(FIELDS):
        turned[16 * f : 16 * f + 8] = lo_recv[8 * f : 8 * f + 8] * has_lo
        turned[16 * f + 8 : 16 * f + 16] = hi_recv[8 * f : 8 * f + 8] * has_hi
    turned[16 * FIELDS :] = jnp.zeros((TILE - 16 * FIELDS, TILE), f32)
    middle = turned[...].T
    short = lax.broadcasted_iota(jnp.int32, (8, TILE), 1) % 16 < 8
    ends = [
        jnp.where(short, dg_recv[side, 0] * has_lo, dg_recv[side, 1] * has_hi) for side in range(2)
    ]
    edges = jnp.concatenate([ends[0], middle, ends[1]], axis=0)
    fields = []
    for f in range(FIELDS):
        core = jnp.concatenate([lf_recv[f], cores[f], rt_recv[f]], axis=0)
        edge = pltpu.roll(edges, TILE - (16 * f + 8), 1)
        fields.append(jnp.concatenate([core, edge], axis=1))

    h, u, v = stencil(fields, la, (cos, sec, coriolis, semi, diurnal), tide)
    h = h[MARGIN : MARGIN + TILE, 0:TILE]
    wet_h = wet_core * h

    sum_send[...] = jnp.sum(wet_h, axis=0, keepdims=True)
    sum_recv[pl.ds(la, 1)] = sum_send[...][None]

    def send_sum(j, carry):
        pltpu.make_async_remote_copy(
            src_ref=sum_send, dst_ref=sum_recv.at[la], send_sem=many_send.at[0],
            recv_sem=many_recv.at[0], device_id=at(la + j, lo), device_id_type=MESH,
        ).start()
        return carry

    lax.fori_loop(1, LATS, send_sum, 0)
    wet_h_t = wet_h.T
    for s in range(LONS):
        a1s[s] = wet_h_t[ROWS * s : ROWS * s + ROWS]
    exchange(1, a1s, a1r)
    h_out[...] = h
    u_out[...] = u[MARGIN : MARGIN + TILE, 0:TILE]
    v_out[...] = v[MARGIN : MARGIN + TILE, 0:TILE]

    def analyse(spectra):
        cos_t = twist[0:32]
        sin_t = twist[32:64]
        blocks = []
        for l in range(ROWS):
            re = spectra[64 * l : 64 * l + 32]
            im = spectra[64 * l + 32 : 64 * l + 64]
            blocks.append(
                jnp.concatenate([re * cos_t + im * sin_t, im * cos_t - re * sin_t], axis=1)
            )
        return across(second[...], halves(jnp.concatenate(blocks, axis=0), 1))

    for load in loads[9:12]:
        load.wait()
    take(many_recv, 7, a0r, LONS - 1)
    mask_rows = rows_of(a0r).astype(bf16)
    full = analyse(
        jnp.dot(
            first[:, TILE:], jnp.concatenate([mask_rows, mask_rows], axis=0), preferred_element_type=f32
        )
    )
    for s in range(LONS):
        aws[s] = full[SLOTS * s : SLOTS * s + SLOTS]
    exchange(8, aws, awr)
    take(many_recv, 1, a1r, LONS - 1)
    full = analyse(jnp.dot(first[...], halves(rows_of(a1r), 0), preferred_element_type=f32))
    for s in range(LONS):
        a2s[s] = full[SLOTS * s : SLOTS * s + SLOTS]
    take(many_recv, 0, sum_recv, LATS - 1)
    band_sum = jnp.sum(sum_recv[...], axis=0)
    kind_row = lax.broadcasted_iota(jnp.int32, (TILE, TILE), 0) % SLOTS
    for s in range(LONS):
        a2s[s, 2:3] = band_sum
    exchange(2, a2s, a2r)
    for load in loads[12:15]:
        load.wait()
    count = jnp.sum(counts_ref[...].astype(f32), keepdims=True)
    take(many_recv, 8, awr, LONS - 1)
    got_mask = rows_of(awr)
    take(many_recv, 2, a2r, LONS - 1)
    got = rows_of(a2r)
    total = jnp.sum(jnp.where(kind_row == 2, got, 0.0), keepdims=True)
    fourier = (got - (total / count) * got_mask).astype(bf16)
    placed = lax.dot_general(
        fourier, place[...], (((0,), (0,)), ((), ())), preferred_element_type=f32
    )
    waves_r = []
    for r in range(2):
        value = placed[0:32, 128 * r : 128 * r + 128]
        for l in range(1, ROWS):
            start = 256 * l + 128 * r
            value = value + placed[32 * l : 32 * l + 32, start : start + 128]
        waves_r.append(value)

    sub = lax.broadcasted_iota(jnp.int32, (16, TILE), 0) % 8
    for g in range(4):
        pair = jnp.concatenate([waves_r[0][8 * g : 8 * g + 8], waves_r[1][8 * g : 8 * g + 8]], axis=0)
        for j in range(8):
            lhs_ref[g, :, TILE * j : TILE * j + TILE] = jnp.where(sub == j, pair, 0.0).astype(bf16)

    near = la % 2
    y_own = la // 2

    def y_at(t):
        return (y_own + 2 + t - t // 2 * (2 * t - 1)) % 4

    def analysis(t, carry):
        y = y_at(t)
        start = pl.multiple_of(y * QUARTER, QUARTER)
        for g in range(4):
            rhs = jnp.concatenate([leg[8 * g + j, pl.ds(start, QUARTER), :] for j in range(8)], axis=1)
            acc = across(lhs_ref[g], rhs)
            cs[y, 16 * g : 16 * g + 16] = acc
            cb[y, 16 * g : 16 * g + 16] = acc.astype(bf16)
        pltpu.make_async_remote_copy(
            src_ref=cb.at[y], dst_ref=db.at[y_own], send_sem=many_send.at[9],
            recv_sem=many_recv.at[9], device_id=at(2 * y + 1 - near, lo), device_id_type=MESH,
        ).start()

        @pl.when(t != 3)
        def _():
            pltpu.make_async_remote_copy(
                src_ref=cs.at[y], dst_ref=cr.at[y_own], send_sem=many_send.at[3],
                recv_sem=many_recv.at[3], device_id=at(2 * y + near, lo), device_id_type=MESH,
            ).start()

        return carry

    lax.fori_loop(0, 4, analysis, 0)
    cr[pl.ds(y_own, 1)] = cs[pl.ds(y_own, 1)]
    love = jnp.concatenate([love_ref[pl.ds(2 * y_own, 1)], love_ref[pl.ds(2 * y_own + 1, 1)]], axis=1)
    take(many_recv, 3, cr, 3)
    coefficients = jnp.sum(cr[...], axis=0)
    take(many_recv, 9, db, 4)
    coefficients = coefficients + jnp.sum(db[...].astype(f32), axis=0)
    sg[pl.ds(y_own, 1)] = (coefficients * love).astype(bf16)[None]

    def send_scaled(t, carry):
        pltpu.make_async_remote_copy(
            src_ref=sg.at[y_own], dst_ref=sg.at[y_own], send_sem=many_send.at[4],
            recv_sem=scaled_recv.at[y_own], device_id=at(2 * y_at(t) + near, lo), device_id_type=MESH,
        ).start()
        return carry

    lax.fori_loop(0, 3, send_scaled, 0)
    for load in loads[15:]:
        load.wait()

    def take_scaled(owner):
        part = sg.at[owner]
        pltpu.make_async_copy(part, part, scaled_recv.at[owner]).wait()

    def synthesis(t, carry):
        owner = y_at(3 - t)

        @pl.when(t != 0)
        def _():
            take_scaled(owner)

        start = pl.multiple_of(owner * QUARTER, QUARTER)
        scaled = sg[owner]
        for g in range(4):
            lhs = scaled[16 * g : 16 * g + 16]
            for k in range(4):
                rhs = jnp.concatenate(
                    [leg[8 * g + 2 * k + i, pl.ds(start, QUARTER), :] for i in range(2)], axis=1
                )
                acc_ref[4 * g + k] += jnp.dot(lhs, rhs, preferred_element_type=f32)
        return carry

    acc_ref[...] = jnp.zeros((16, 16, 256), f32)
    lax.fori_loop(0, 4, synthesis, 0)
    heads = []
    for g in range(4):
        acc = jnp.zeros((16, TILE), f32)
        for k in range(4):
            acc = jnp.where(sub == 2 * k, acc_ref[4 * g + k, :, 0:TILE], acc)
            acc = jnp.where(sub == 2 * k + 1, acc_ref[4 * g + k, :, TILE:], acc)
        if g == 0:
            weight = jnp.where((sub == 0) & (lo == 0), 1.0 / 64.0, 2.0 / 64.0)
            acc = acc * weight
        else:
            acc = acc * (2.0 / 64.0)
        heads.append(acc)
    both = jnp.concatenate(
        [
            jnp.concatenate([heads[g][0:8] for g in range(4)], axis=0),
            jnp.concatenate([heads[g][8:16] for g in range(4)], axis=0),
        ],
        axis=1,
    )
    empty = jnp.zeros((WAVES, 256), f32)
    stacked = jnp.concatenate(
        [
            jnp.concatenate([both if c == l else empty for c in range(ROWS)], axis=1)
            for l in range(ROWS)
        ],
        axis=0,
    )
    rows = across(spread[...], stacked.astype(bf16))
    a3s[...] = rows.astype(bf16).reshape(8, 8, TILE)

    def send_rows(peer):
        pltpu.make_async_remote_copy(
            src_ref=a3s.at[peer % 8], dst_ref=a3r.at[lo], send_sem=many_send.at[5],
            recv_sem=many_recv.at[5], device_id=at(la, peer), device_id_type=MESH,
        ).start()

    for dx in (2, 1, 3, 0):

        def send_block(j, carry, dx=dx):
            send_rows((lo // 8 + dx) % 4 * 8 + (lo + j) % 8)
            return carry

        lax.fori_loop(1 if dx == 0 else 0, 8, send_block, 0)
    a3r[pl.ds(lo, 1)] = a3s[pl.ds(lo % 8, 1)]
    take(many_recv, 5, a3r, LONS - 1)

    every = a3r[...].reshape(256, TILE)
    opened = jnp.dot(back[...], jnp.concatenate([every, every], axis=0), preferred_element_type=f32)
    cos_u = untwist[0]
    sin_u = untwist[1]
    mine = last[pl.ds(pl.multiple_of(lo // 8 * 32, 32), 32), :]
    for quad in range(4):
        re = opened[256 * quad : 256 * quad + TILE]
        im = opened[256 * quad + TILE : 256 * quad + 256]
        untwisted = jnp.concatenate([re * cos_u - im * sin_u, re * sin_u + im * cos_u], axis=1)
        field = across(mine, halves(untwisted, 1))
        for e in range(8):
            a4s[e, 4 * quad : 4 * quad + 4] = field[4 * e : 4 * e + 4]

    def send_field(j, carry):
        e = (lo + j) % 8
        pltpu.make_async_remote_copy(
            src_ref=a4s.at[e], dst_ref=a4r.at[lo % 8], send_sem=many_send.at[6],
            recv_sem=many_recv.at[6], device_id=at(la, lo // 8 * 8 + e), device_id_type=MESH,
        ).start()
        return carry

    lax.fori_loop(1, 8, send_field, 0)
    a4r[pl.ds(lo % 8, 1)] = a4s[pl.ds(lo % 8, 1)]
    take(many_recv, 6, a4r, 7)
    s_out[...] = a4r[...].reshape(TILE, TILE).T

    for move in halo:
        move.wait_send()
    take(many_send, 0, sum_recv, LATS - 1)
    take(many_send, 1, a1s, LONS - 1)
    take(many_send, 2, a2s, LONS - 1)
    take(many_send, 3, cs, 3)
    take(many_send, 9, cb, 4)
    take(many_send, 4, sg, 3)
    take(many_send, 5, a3r, LONS - 1)
    take(many_send, 6, a4s, 7)
    take(many_send, 7, a0s, LONS - 1)
    take(many_send, 8, aws, LONS - 1)


def deliver(*refs):
    sems = refs[-1]
    copies = [pltpu.make_async_copy(refs[i], refs[i + 4], sems.at[i]) for i in range(4)]
    for copy in copies:
        copy.start()
    for copy in copies:
        copy.wait()


def shards(
    sea_level, east_velocity, north_velocity, depth, land_mask, wet_counts, loading_prev,
    tide_amp, tide_phase, legendre, love_factor,
):
    tables = make_tables()
    hbm = pl.BlockSpec(memory_space=pltpu.HBM)
    vmem = pl.BlockSpec(memory_space=pltpu.VMEM)
    shape = jax.ShapeDtypeStruct((TILE, TILE), f32)
    tile = pltpu.VMEM((TILE, TILE), f32)
    slab = pltpu.VMEM((FIELDS, 8, TILE), f32)
    edge = pltpu.VMEM((48, TILE), f32)
    quad = pltpu.VMEM((LONS, SLOTS, TILE), f32)
    part = pltpu.VMEM((4, 64, QUARTER), f32)
    rough = pltpu.VMEM((4, 64, QUARTER), bf16)
    scratch = [tile, tile, tile, tile, pltpu.VMEM((TILE, TILE), jnp.int32), tile]
    scratch += [pltpu.SMEM((8,), f32), pltpu.SMEM((8,), f32)]
    scratch += [pltpu.VMEM((LATS, LONS), jnp.int32), pltpu.VMEM((LATS, TILE), f32)]
    scratch += [pltpu.VMEM((WAVES, NDEG, TILE), bf16)]
    scratch += [pltpu.VMEM(x.shape, x.dtype) for x in tables]
    scratch += [edge, edge, edge, edge, slab, slab, slab, slab]
    scratch += [pltpu.VMEM((2, 8, TILE), f32), pltpu.VMEM((2, 2, 8, TILE), f32), tile]
    scratch += [pltpu.VMEM((1, TILE), f32), pltpu.VMEM((LATS, 1, TILE), f32)]
    scratch += [quad] * 8
    scratch += [pltpu.VMEM((4, 16, 8 * TILE), bf16), part, part, rough, rough, rough]
    scratch += [pltpu.VMEM((16, 16, 2 * TILE), f32), pltpu.VMEM((8, 8, TILE), bf16)]
    scratch += [pltpu.VMEM((LONS, 8, TILE), bf16)] + [pltpu.VMEM((8, 16, TILE), f32)] * 2
    scratch += [
        pltpu.SemaphoreType.DMA((19,)),
        pltpu.SemaphoreType.DMA((8,)), pltpu.SemaphoreType.DMA((8,)),
        pltpu.SemaphoreType.DMA((10,)), pltpu.SemaphoreType.DMA((10,)), pltpu.SemaphoreType.DMA((4,)),
    ]
    results = pl.pallas_call(
        kernel,
        out_shape=(shape,) * 4,
        in_specs=[hbm] * 19,
        out_specs=(vmem,) * 4,
        scratch_shapes=scratch,
        compiler_params=pltpu.CompilerParams(
            collective_id=0, has_side_effects=True, vmem_limit_bytes=VMEM_BYTES
        ),
        name="tide",
    )(
        *[
            pltpu.with_memory_space_constraint(x, pltpu.HBM)
            for x in (
                sea_level, east_velocity, north_velocity, depth, land_mask, loading_prev, tide_amp,
                tide_phase, wet_counts, love_factor.reshape(LATS, NDEG // LATS), legendre,
                *[jnp.asarray(x) for x in tables],
            )
        ]
    )
    return pl.pallas_call(
        deliver,
        out_shape=(shape,) * 4,
        in_specs=[pl.BlockSpec(memory_space=pl.ANY)] * 4,
        out_specs=(hbm,) * 4,
        scratch_shapes=[pltpu.SemaphoreType.DMA((4,))],
        compiler_params=pltpu.CompilerParams(vmem_limit_bytes=1024 * 1024),
        name="deliver",
    )(*results)


def solution(mesh):
    grid = P("lon", "lat")
    return jax.shard_map(
        shards,
        mesh=mesh,
        in_specs=(grid, grid, grid, grid, grid, P(), grid, P(), P(), P("lon", None, "lat"), P()),
        out_specs=(grid, grid, grid, grid),
        check_vma=False,
    )
```

```python
import functools
import math

import jax
import jax.numpy as jnp
import ml_dtypes
import numpy as np
from jax import lax
from jax.experimental import pallas as pl
from jax.experimental.pallas import tpu as pltpu
from jax.sharding import PartitionSpec as P

SUBSTEPS = 4
NLON = 4096
NLAT = 1024
NDEG = 1024
LONS = 32
LATS = 8
TILE = 128
WAVES = 32
ROWS = TILE // LONS
MARGIN = 8
WIDE = TILE + 2 * MARGIN
FIELDS = 6
SLOTS = 4
QUARTER = NDEG // 4
VMEM_BYTES = 40 * 1024 * 1024

lat_edge = 1.3089969
courant = 0.4
friction = 0.02
rotation = 0.2
frequencies = (0.1405, 0.1454, 0.1379, 0.1458, 0.0729, 0.0676, 0.0725, 0.0649)
orders = (2, 2, 2, 2, 1, 1, 1, 1)
highest = lax.Precision.HIGHEST
MESH = pl.DeviceIdType.MESH
f32 = jnp.float32
bf16 = jnp.bfloat16


def turn(product, period):
    angle = 2.0 * np.pi * (product % period) / period
    return np.cos(angle), np.sin(angle)


def split(table):
    high = table.astype(ml_dtypes.bfloat16)
    low = (table - high.astype(np.float64)).astype(ml_dtypes.bfloat16)
    return np.concatenate([high, high, low], axis=1)


def make_tables():
    band = np.arange(32)
    cell = np.arange(128)
    cos, sin = turn(np.outer(band, band), 32)
    first = np.zeros((ROWS, 2, 32, 32, ROWS))
    for row in range(ROWS):
        first[row, 0, :, :, row] = cos
        first[row, 1, :, :, row] = -sin
    first = first.reshape(256, 128)
    cos, sin = turn(np.outer(band, cell), 4096)
    extra = np.zeros((8, 128))
    extra[0, :32] = (np.arange(SUBSTEPS)[:, None] * np.array(frequencies)[None, :]).reshape(-1)
    extra[1, :32] = np.tile(np.array(orders), SUBSTEPS)
    twist = np.concatenate([cos, sin, extra])
    cos, sin = turn(np.outer(band, cell), 128)
    second = np.zeros((32, SLOTS, 2, 128))
    second[:, 0, 0] = cos / 64.0
    second[:, 0, 1] = sin / 64.0
    second[:, 1, 0] = -sin / 64.0
    second[:, 1, 1] = cos / 64.0
    second = second.reshape(128, 256)
    place = np.zeros((32, SLOTS, ROWS, 2, 128))
    for s in range(32):
        for row in range(ROWS):
            for r in range(2):
                place[s, r, row, r, ROWS * s + row] = 1.0
    spread = place[:, :2].reshape(8, 4, 2, 1024).transpose(0, 2, 1, 3).reshape(64, 1024)
    place = place.reshape(128, 1024)
    cos, sin = turn(np.outer(cell, band), 128)
    back = np.zeros((4, 2, 128, 32, 2, 4))
    for quad in range(4):
        back[quad, 0, :, :, 0, quad] = cos
        back[quad, 0, :, :, 1, quad] = -sin
        back[quad, 1, :, :, 0, quad] = sin
        back[quad, 1, :, :, 1, quad] = cos
    back = back.reshape(1024, 256)
    cos, sin = turn(np.outer(cell, band), 4096)
    untwist = np.stack([np.tile(cos, (1, ROWS)), np.tile(sin, (1, ROWS))])
    cos, sin = turn(np.outer(band, band), 32)
    last = np.zeros((32, ROWS, 2, ROWS, 32))
    for row in range(ROWS):
        last[:, row, 0, row, :] = cos
        last[:, row, 1, row, :] = -sin
    last = last.reshape(128, 256)
    plain = [x.astype(np.float32) for x in (twist, untwist)]
    exact = [x.astype(ml_dtypes.bfloat16) for x in (place, spread)]
    return [split(first), plain[0], split(second), exact[0], split(back)[:, 256:], plain[1], split(last), exact[1]]


def halves(value, axis):
    high = value.astype(bf16)
    low = (value - high.astype(f32)).astype(bf16)
    return jnp.concatenate([high, low, high], axis=axis)


def stencil(fields, la, north_table, tide):
    h, u, v, depth, wet, loading = fields
    cos, sec, coriolis, semi, diurnal = north_table

    def up(x, axis):
        return pltpu.roll(x, x.shape[axis] - 1, axis)

    def down(x, axis):
        return pltpu.roll(x, 1, axis)

    for moment in range(SUBSTEPS):
        forcing = semi * tide[moment][0] + diurnal * tide[moment][1]
        flux_east = depth * u
        flux_north = depth * v * cos
        divergence = (
            (up(flux_east, 0) - down(flux_east, 0) + (up(flux_north, 1) - down(flux_north, 1)))
            * 0.5
            * sec
        )
        h = h - courant * divergence * wet
        pressure = h - forcing - loading
        slope_east = (up(pressure, 0) - down(pressure, 0)) * 0.5 * sec
        slope_north = (up(pressure, 1) - down(pressure, 1)) * 0.5
        u, v = (
            wet * ((1.0 - friction) * u + courant * (coriolis * v - slope_east)),
            wet * ((1.0 - friction) * v - courant * (coriolis * u + slope_north)),
        )
    return h, u, v


def across(lhs, rhs):
    return lax.dot_general(lhs, rhs, (((1,), (1,)), ((), ())), preferred_element_type=f32)


def kernel(
    sea_hbm, east_hbm, north_hbm, depth_hbm, mask_hbm, load_hbm, amp_hbm, phase_hbm, counts_hbm, love_hbm,
    leg_hbm, first_hbm, twist_hbm, second_hbm, place_hbm, back_hbm, untwist_hbm, last_hbm, spread_hbm,
    h_out, u_out, v_out, s_out,
    sea_ref, east_ref, north_ref, depth_ref, mask_ref, load_ref, amp_ref, phase_ref, counts_ref, love_ref,
    leg, first, twist, second, place, back, untwist, last, spread,
    up_send, dn_send, lo_recv, hi_recv, lf_send, rt_send, lf_recv, rt_recv, dg_send, dg_recv, turned,
    sum_send, sum_recv, a0s, a0r, a1s, a1r, aws, awr, a2s, a2r, lhs_ref, cs, cr, cb, db, sg, acc_ref, a3s, a3r, a4s, a4r,
    local_sem, halo_send, halo_recv, many_send, many_recv, scaled_recv,
):
    la = lax.axis_index("lat")
    lo = lax.axis_index("lon")

    def at(lat, lon):
        return {"lat": lat % LATS, "lon": lon % LONS}

    pairs = (
        (sea_hbm, sea_ref), (east_hbm, east_ref), (north_hbm, north_ref), (depth_hbm, depth_ref),
        (mask_hbm, mask_ref), (load_hbm, load_ref), (amp_hbm, amp_ref), (phase_hbm, phase_ref),
        (twist_hbm, twist), (first_hbm, first), (second_hbm, second), (place_hbm, place),
        (counts_hbm, counts_ref), (leg_hbm, leg), (love_hbm, love_ref.at[pl.ds(0, LATS)]), (spread_hbm, spread),
        (back_hbm, back), (untwist_hbm, untwist), (last_hbm, last),
    )
    loads = [
        pltpu.make_async_copy(src, dst, local_sem.at[i]) for i, (src, dst) in enumerate(pairs)
    ]
    barrier = pltpu.get_barrier_semaphore()

    def greet_lon(j, carry):
        pl.semaphore_signal(barrier, inc=1, device_id=at(la, lo + j), device_id_type=MESH)
        return carry

    def greet_lat(j, carry):
        pl.semaphore_signal(barrier, inc=1, device_id=at(la + j, lo), device_id_type=MESH)
        return carry

    lax.fori_loop(1, LATS, greet_lat, 0)
    for dl in (1, LATS - 1):
        for dn in (1, LONS - 1):
            pl.semaphore_signal(barrier, inc=1, device_id=at(la + dl, lo + dn), device_id_type=MESH)
    for load in loads[0:6]:
        load.start()
    lax.fori_loop(1, LONS, greet_lon, 0)
    for load in loads[6:]:
        load.start()
    for load in loads[0:6]:
        load.wait()

    wet_core = mask_ref[...].astype(f32)
    cores = [sea_ref[...], east_ref[...], north_ref[...], depth_ref[...], wet_core, load_ref[...]]
    lane = lax.broadcasted_iota(jnp.int32, (TILE, TILE), 1)
    packed = jnp.zeros((TILE, TILE), f32)
    for f in range(FIELDS):
        moved = pltpu.roll(cores[f], 16 * f + 8, 1)
        packed = jnp.where((lane >= 16 * f) & (lane < 16 * f + 16), moved, packed)
        lf_send[f] = cores[f][0:8]
        rt_send[f] = cores[f][TILE - 8 : TILE]
    dg_send[0] = packed[0:8]
    dg_send[1] = packed[TILE - 8 : TILE]
    packed_t = packed.T
    for f in range(FIELDS):
        up_send[8 * f : 8 * f + 8] = packed_t[16 * f : 16 * f + 8]
        dn_send[8 * f : 8 * f + 8] = packed_t[16 * f + 8 : 16 * f + 16]
    wet_t = wet_core.T
    for s in range(LONS):
        a0s[s] = wet_t[ROWS * s : ROWS * s + ROWS]

    slot = lax.broadcasted_iota(jnp.int32, (1, 2 * TILE), 1)
    row = la * TILE + jnp.where(slot < 192, slot, slot - 256)
    phi = -lat_edge + 2.0 * lat_edge * (row.astype(f32) + 0.5) / NLAT
    phi = jnp.clip(phi, -1.5, 1.5)
    cos = jnp.cos(phi)
    sec = 1.0 / cos
    coriolis = rotation * jnp.sin(phi)
    semi = cos * cos * (NLON / 64.0)
    diurnal = jnp.sin(2.0 * phi) * (NLON / 64.0)
    for load in loads[6:9]:
        load.wait()
    short_lane = lax.broadcasted_iota(jnp.int32, (1, TILE), 1)
    amp = jnp.zeros((1, TILE), f32)
    phase = jnp.zeros((1, TILE), f32)
    for c in range(8):
        hit = (short_lane % 8 == c) & (short_lane < 8 * SUBSTEPS)
        amp = jnp.where(hit, amp_ref[c], amp)
        phase = jnp.where(hit, phase_ref[c], phase)
    phase = phase + twist[64:65]
    column = lo * TILE + lax.broadcasted_iota(jnp.int32, (WIDE, TILE), 0) + (NLON - MARGIN)
    lam = 2.0 * math.pi * (column % NLON).astype(f32) / NLON
    waves = amp * jnp.cos(twist[65:66] * lam + phase)
    wide_lane = lax.broadcasted_iota(jnp.int32, (WIDE, TILE), 1)
    tide = []
    for moment in range(SUBSTEPS):
        pair = []
        for kind in range(2):
            low = 8 * moment + 4 * kind
            inside = (wide_lane >= low) & (wide_lane < low + 4)
            pair.append(jnp.sum(jnp.where(inside, waves, 0.0), axis=1, keepdims=True))
        tide.append(pair)

    pl.semaphore_wait(barrier, LONS - 1 + LATS - 1 + 4)

    moves = (
        (dg_send.at[0], dg_recv.at[1, 0], at(la + 1, lo + LONS - 1)),
        (dg_send.at[0], dg_recv.at[1, 1], at(la + LATS - 1, lo + LONS - 1)),
        (dg_send.at[1], dg_recv.at[0, 0], at(la + 1, lo + 1)),
        (dg_send.at[1], dg_recv.at[0, 1], at(la + LATS - 1, lo + 1)),
        (up_send, lo_recv, at(la + 1, lo)),
        (dn_send, hi_recv, at(la + LATS - 1, lo)),
        (lf_send, rt_recv, at(la, lo + LONS - 1)),
        (rt_send, lf_recv, at(la, lo + 1)),
    )
    halo = [
        pltpu.make_async_remote_copy(
            src_ref=src, dst_ref=dst, send_sem=halo_send.at[i], recv_sem=halo_recv.at[i],
            device_id=dev, device_id_type=MESH,
        )
        for i, (src, dst, dev) in enumerate(moves)
    ]
    for move in halo:
        move.start()

    def exchange(index, source, target):
        def one(peer):
            pltpu.make_async_remote_copy(
                src_ref=source.at[peer], dst_ref=target.at[lo], send_sem=many_send.at[index],
                recv_sem=many_recv.at[index], device_id=at(la, peer), device_id_type=MESH,
            ).start()

        for dx in (2, 1, 3, 0):

            def send(j, carry, dx=dx):
                one((lo // 8 + dx) % 4 * 8 + (lo + j) % 8)
                return carry

            lax.fori_loop(1 if dx == 0 else 0, 8, send, 0)
        target[pl.ds(lo, 1)] = source[pl.ds(lo, 1)]

    def take(sems, index, buffer, count):
        part = buffer.at[pl.ds(0, count)]
        pltpu.make_async_copy(part, part, sems.at[index]).wait()

    def rows_of(buffer):
        return jnp.concatenate([buffer[s] for s in range(LONS)], axis=0)

    for move in halo[6:]:
        move.wait_recv()
    exchange(7, a0s, a0r)
    for move in halo[0:6]:
        move.wait_recv()

    has_lo = jnp.where(la > 0, 1.0, 0.0).astype(f32)
    has_hi = jnp.where(la < LATS - 1, 1.0, 0.0).astype(f32)
    for f in range(FIELDS):
        turned[16 * f : 16 * f + 8] = lo_recv[8 * f : 8 * f + 8] * has_lo
        turned[16 * f + 8 : 16 * f + 16] = hi_recv[8 * f : 8 * f + 8] * has_hi
    turned[16 * FIELDS :] = jnp.zeros((TILE - 16 * FIELDS, TILE), f32)
    middle = turned[...].T
    short = lax.broadcasted_iota(jnp.int32, (8, TILE), 1) % 16 < 8
    ends = [
        jnp.where(short, dg_recv[side, 0] * has_lo, dg_recv[side, 1] * has_hi) for side in range(2)
    ]
    edges = jnp.concatenate([ends[0], middle, ends[1]], axis=0)
    fields = []
    for f in range(FIELDS):
        core = jnp.concatenate([lf_recv[f], cores[f], rt_recv[f]], axis=0)
        edge = pltpu.roll(edges, TILE - (16 * f + 8), 1)
        fields.append(jnp.concatenate([core, edge], axis=1))

    h, u, v = stencil(fields, la, (cos, sec, coriolis, semi, diurnal), tide)
    h = h[MARGIN : MARGIN + TILE, 0:TILE]
    wet_h = wet_core * h

    own_sum = jnp.sum(wet_h, axis=0, keepdims=True)
    sum_send[0] = own_sum
    sum_recv[pl.ds(la, 1)] = own_sum[None]

    def send_sum(j, carry):
        pltpu.make_async_remote_copy(
            src_ref=sum_send.at[0], dst_ref=sum_recv.at[la], send_sem=many_send.at[0],
            recv_sem=many_recv.at[0], device_id=at(la + j, lo), device_id_type=MESH,
        ).start()
        return carry

    lax.fori_loop(1, LATS, send_sum, 0)
    wet_h_t = wet_h.T
    for s in range(LONS):
        a1s[s] = wet_h_t[ROWS * s : ROWS * s + ROWS]
    exchange(1, a1s, a1r)
    h_out[...] = h
    u_out[...] = u[MARGIN : MARGIN + TILE, 0:TILE]
    v_out[...] = v[MARGIN : MARGIN + TILE, 0:TILE]

    def analyse(spectra):
        cos_t = twist[0:32]
        sin_t = twist[32:64]
        blocks = []
        for l in range(ROWS):
            re = spectra[64 * l : 64 * l + 32]
            im = spectra[64 * l + 32 : 64 * l + 64]
            blocks.append(
                jnp.concatenate([re * cos_t + im * sin_t, im * cos_t - re * sin_t], axis=1)
            )
        return across(second[...], halves(jnp.concatenate(blocks, axis=0), 1))

    for load in loads[9:12]:
        load.wait()
    take(many_recv, 7, a0r, LONS - 1)
    mask_rows = rows_of(a0r).astype(bf16)
    full = analyse(
        jnp.dot(
            first[:, TILE:], jnp.concatenate([mask_rows, mask_rows], axis=0), preferred_element_type=f32
        )
    )
    for s in range(LONS):
        aws[s] = full[SLOTS * s : SLOTS * s + SLOTS]
    exchange(8, aws, awr)
    take(many_recv, 1, a1r, LONS - 1)
    full = analyse(jnp.dot(first[...], halves(rows_of(a1r), 0), preferred_element_type=f32))
    for s in range(LONS):
        a2s[s] = full[SLOTS * s : SLOTS * s + SLOTS]
    take(many_recv, 0, sum_recv, LATS - 1)
    band_sum = jnp.sum(sum_recv[0:LATS], axis=0)
    kind_row = lax.broadcasted_iota(jnp.int32, (TILE, TILE), 0) % SLOTS
    for s in range(LONS):
        a2s[s, 2:3] = band_sum
    exchange(2, a2s, a2r)
    for load in loads[12:15]:
        load.wait()
    count = jnp.sum(counts_ref[...].astype(f32), keepdims=True)
    take(many_recv, 8, awr, LONS - 1)
    got_mask = rows_of(awr)
    take(many_recv, 2, a2r, LONS - 1)
    got = rows_of(a2r)
    total = jnp.sum(jnp.where(kind_row == 2, got, 0.0), keepdims=True)
    fourier = (got - (total / count) * got_mask).astype(bf16)
    placed = lax.dot_general(
        fourier, place[...], (((0,), (0,)), ((), ())), preferred_element_type=f32
    )
    waves_r = []
    for r in range(2):
        value = placed[0:32, 128 * r : 128 * r + 128]
        for l in range(1, ROWS):
            start = 256 * l + 128 * r
            value = value + placed[32 * l : 32 * l + 32, start : start + 128]
        waves_r.append(value)

    sub = lax.broadcasted_iota(jnp.int32, (16, TILE), 0) % 8
    for g in range(4):
        pair = jnp.concatenate([waves_r[0][8 * g : 8 * g + 8], waves_r[1][8 * g : 8 * g + 8]], axis=0)
        for j in range(8):
            lhs_ref[g, :, TILE * j : TILE * j + TILE] = jnp.where(sub == j, pair, 0.0).astype(bf16)

    near = la % 2
    y_own = la // 2

    def y_at(t):
        return (y_own + 2 + t - t // 2 * (2 * t - 1)) % 4

    def analysis(t, carry):
        y = y_at(t)
        start = pl.multiple_of(y * QUARTER, QUARTER)
        for g in range(4):
            rhs = jnp.concatenate([leg[8 * g + j, pl.ds(start, QUARTER), :] for j in range(8)], axis=1)
            acc = across(lhs_ref[g], rhs)
            cs[y, 16 * g : 16 * g + 16] = acc
            cb[y, 16 * g : 16 * g + 16] = acc.astype(bf16)
        pltpu.make_async_remote_copy(
            src_ref=cb.at[y], dst_ref=db.at[y_own], send_sem=many_send.at[9],
            recv_sem=many_recv.at[9], device_id=at(2 * y + 1 - near, lo), device_id_type=MESH,
        ).start()

        @pl.when(t != 3)
        def _():
            pltpu.make_async_remote_copy(
                src_ref=cs.at[y], dst_ref=cr.at[y_own], send_sem=many_send.at[3],
                recv_sem=many_recv.at[3], device_id=at(2 * y + near, lo), device_id_type=MESH,
            ).start()

        return carry

    lax.fori_loop(0, 4, analysis, 0)
    cr[pl.ds(y_own, 1)] = cs[pl.ds(y_own, 1)]
    love = jnp.concatenate([love_ref[pl.ds(2 * y_own, 1)], love_ref[pl.ds(2 * y_own + 1, 1)]], axis=1)
    take(many_recv, 3, cr, 3)
    coefficients = jnp.sum(cr[...], axis=0)
    take(many_recv, 9, db, 4)
    coefficients = coefficients + jnp.sum(db[...].astype(f32), axis=0)
    sg[pl.ds(y_own, 1)] = (coefficients * love).astype(bf16)[None]

    def send_scaled(t, carry):
        pltpu.make_async_remote_copy(
            src_ref=sg.at[y_own], dst_ref=sg.at[y_own], send_sem=many_send.at[4],
            recv_sem=scaled_recv.at[y_own], device_id=at(2 * y_at(t) + near, lo), device_id_type=MESH,
        ).start()
        return carry

    lax.fori_loop(0, 3, send_scaled, 0)
    for load in loads[15:]:
        load.wait()

    def take_scaled(owner):
        part = sg.at[owner]
        pltpu.make_async_copy(part, part, scaled_recv.at[owner]).wait()

    def synthesis(t, carry):
        owner = y_at(3 - t)

        @pl.when(t != 0)
        def _():
            take_scaled(owner)

        start = pl.multiple_of(owner * QUARTER, QUARTER)
        scaled = sg[owner]
        for g in range(4):
            lhs = scaled[16 * g : 16 * g + 16]
            for k in range(4):
                rhs = jnp.concatenate(
                    [leg[8 * g + 2 * k + i, pl.ds(start, QUARTER), :] for i in range(2)], axis=1
                )
                acc_ref[4 * g + k] += jnp.dot(lhs, rhs, preferred_element_type=f32)
        return carry

    acc_ref[...] = jnp.zeros((16, 16, 256), f32)
    lax.fori_loop(0, 4, synthesis, 0)
    heads = []
    for g in range(4):
        acc = jnp.zeros((16, TILE), f32)
        for k in range(4):
            acc = jnp.where(sub == 2 * k, acc_ref[4 * g + k, :, 0:TILE], acc)
            acc = jnp.where(sub == 2 * k + 1, acc_ref[4 * g + k, :, TILE:], acc)
        if g == 0:
            weight = jnp.where((sub == 0) & (lo == 0), 1.0 / 64.0, 2.0 / 64.0)
            acc = acc * weight
        else:
            acc = acc * (2.0 / 64.0)
        heads.append(acc)
    both = jnp.concatenate(
        [
            jnp.concatenate([heads[g][0:8] for g in range(4)], axis=0),
            jnp.concatenate([heads[g][8:16] for g in range(4)], axis=0),
        ],
        axis=1,
    )
    empty = jnp.zeros((WAVES, 256), f32)
    stacked = jnp.concatenate(
        [
            jnp.concatenate([both if c == l else empty for c in range(ROWS)], axis=1)
            for l in range(ROWS)
        ],
        axis=0,
    )
    rows = across(spread[...], stacked.astype(bf16))
    a3s[0:8] = rows.astype(bf16).reshape(8, 8, TILE)

    def send_rows(peer):
        pltpu.make_async_remote_copy(
            src_ref=a3s.at[peer % 8], dst_ref=a3r.at[lo], send_sem=many_send.at[5],
            recv_sem=many_recv.at[5], device_id=at(la, peer), device_id_type=MESH,
        ).start()

    for dx in (2, 1, 3, 0):

        def send_block(j, carry, dx=dx):
            send_rows((lo // 8 + dx) % 4 * 8 + (lo + j) % 8)
            return carry

        lax.fori_loop(1 if dx == 0 else 0, 8, send_block, 0)
    a3r[pl.ds(lo, 1)] = a3s[pl.ds(lo % 8, 1)]
    take(many_recv, 5, a3r, LONS - 1)

    every = a3r[0:LONS].reshape(256, TILE)
    opened = jnp.dot(back[...], jnp.concatenate([every, every], axis=0), preferred_element_type=f32)
    cos_u = untwist[0]
    sin_u = untwist[1]
    mine = last[pl.ds(pl.multiple_of(lo // 8 * 32, 32), 32), :]
    for quad in range(4):
        re = opened[256 * quad : 256 * quad + TILE]
        im = opened[256 * quad + TILE : 256 * quad + 256]
        untwisted = jnp.concatenate([re * cos_u - im * sin_u, re * sin_u + im * cos_u], axis=1)
        field = across(mine, halves(untwisted, 1))
        for e in range(8):
            a4s[e, 4 * quad : 4 * quad + 4] = field[4 * e : 4 * e + 4]

    def send_field(j, carry):
        e = (lo + j) % 8
        pltpu.make_async_remote_copy(
            src_ref=a4s.at[e], dst_ref=a4r.at[lo % 8], send_sem=many_send.at[6],
            recv_sem=many_recv.at[6], device_id=at(la, lo // 8 * 8 + e), device_id_type=MESH,
        ).start()
        return carry

    lax.fori_loop(1, 8, send_field, 0)
    a4r[pl.ds(lo % 8, 1)] = a4s[pl.ds(lo % 8, 1)]
    take(many_recv, 6, a4r, 7)
    s_out[...] = a4r[...].reshape(TILE, TILE).T

    for move in halo:
        move.wait_send()
    take(many_send, 0, sum_recv, LATS - 1)
    take(many_send, 1, a1s, LONS - 1)
    take(many_send, 2, a2s, LONS - 1)
    take(many_send, 3, cs, 3)
    take(many_send, 9, cb, 4)
    take(many_send, 4, sg, 3)
    take(many_send, 5, a3r, LONS - 1)
    take(many_send, 6, a4s, 7)
    take(many_send, 7, a0s, LONS - 1)
    take(many_send, 8, aws, LONS - 1)


def deliver(*refs):
    sems = refs[-1]
    copies = [pltpu.make_async_copy(refs[i], refs[i + 4], sems.at[i]) for i in range(4)]
    for copy in copies:
        copy.start()
    for copy in copies:
        copy.wait()


def shards(
    sea_level, east_velocity, north_velocity, depth, land_mask, wet_counts, loading_prev,
    tide_amp, tide_phase, legendre, love_factor,
):
    tables = make_tables()
    hbm = pl.BlockSpec(memory_space=pltpu.HBM)
    vmem = pl.BlockSpec(memory_space=pltpu.VMEM)
    shape = jax.ShapeDtypeStruct((TILE, TILE), f32)
    tile = pltpu.VMEM((TILE, TILE), f32)
    slab = pltpu.VMEM((FIELDS, 8, TILE), f32)
    edge = pltpu.VMEM((48, TILE), f32)
    quad = pltpu.VMEM((LONS + 2, SLOTS, TILE), f32)
    part = pltpu.VMEM((4, 64, QUARTER), f32)
    rough = pltpu.VMEM((4, 64, QUARTER), bf16)
    scratch = [tile, tile, tile, tile, pltpu.VMEM((TILE, TILE), jnp.int32), tile]
    scratch += [pltpu.SMEM((8,), f32), pltpu.SMEM((8,), f32)]
    scratch += [pltpu.VMEM((LATS, LONS), jnp.int32), pltpu.VMEM((2 * LATS, TILE), f32)]
    scratch += [pltpu.VMEM((WAVES, NDEG, TILE), bf16)]
    scratch += [pltpu.VMEM(x.shape, x.dtype) for x in tables]
    scratch += [edge, edge, edge, edge, slab, slab, slab, slab]
    scratch += [pltpu.VMEM((2, 8, TILE), f32), pltpu.VMEM((2, 2, 8, TILE), f32), tile]
    scratch += [pltpu.VMEM((LATS, 1, TILE), f32), pltpu.VMEM((2 * LATS, 1, TILE), f32)]
    scratch += [quad] * 8
    scratch += [pltpu.VMEM((4, 16, 8 * TILE), bf16), part, part, rough, rough, rough]
    scratch += [pltpu.VMEM((16, 16, 2 * TILE), f32), pltpu.VMEM((10, 8, TILE), bf16)]
    scratch += [pltpu.VMEM((LONS + 2, 8, TILE), bf16)] + [pltpu.VMEM((8, 16, TILE), f32)] * 2
    scratch += [
        pltpu.SemaphoreType.DMA((19,)),
        pltpu.SemaphoreType.DMA((8,)), pltpu.SemaphoreType.DMA((8,)),
        pltpu.SemaphoreType.DMA((10,)), pltpu.SemaphoreType.DMA((10,)), pltpu.SemaphoreType.DMA((4,)),
    ]
    results = pl.pallas_call(
        kernel,
        out_shape=(shape,) * 4,
        in_specs=[hbm] * 19,
        out_specs=(vmem,) * 4,
        scratch_shapes=scratch,
        compiler_params=pltpu.CompilerParams(
            collective_id=0, has_side_effects=True, vmem_limit_bytes=VMEM_BYTES
        ),
        name="tide",
    )(
        *[
            pltpu.with_memory_space_constraint(x, pltpu.HBM)
            for x in (
                sea_level, east_velocity, north_velocity, depth, land_mask, loading_prev, tide_amp,
                tide_phase, wet_counts, love_factor.reshape(LATS, NDEG // LATS), legendre,
                *[jnp.asarray(x) for x in tables],
            )
        ]
    )
    return pl.pallas_call(
        deliver,
        out_shape=(shape,) * 4,
        in_specs=[pl.BlockSpec(memory_space=pl.ANY)] * 4,
        out_specs=(hbm,) * 4,
        scratch_shapes=[pltpu.SemaphoreType.DMA((4,))],
        compiler_params=pltpu.CompilerParams(vmem_limit_bytes=1024 * 1024),
        name="deliver",
    )(*results)


def solution(mesh):
    grid = P("lon", "lat")
    return jax.shard_map(
        shards,
        mesh=mesh,
        in_specs=(grid, grid, grid, grid, grid, P(), grid, P(), P(), P("lon", None, "lat"), P()),
        out_specs=(grid, grid, grid, grid),
        check_vma=False,
    )
```
